512 devices in a mesh: grp: 16 (over y, z_lo), feat: 32 (over x, z_hi, core).
Axes of the slice: x: 4, y: 8, z: 8 (z_hi: 4, z_lo: 2; z = z_hi * 2 + z_lo), core: 2. Of those that a mesh axis runs over, the one named last changes fastest.
Arguments:
- points: bfloat16 [131072, 32], P(('grp', 'feat')), may hold values from -6 to 6
- dual_weights: float32 [131072, 64], P(('grp', 'feat')), may hold values from -6 to 6
- velocity: float32 [131072, 64], P(('grp', 'feat')), may hold values from -1.75 to 1.75
- observed: float32 [131072], P(('grp', 'feat')), may hold values from -12 to 12
- noise_draws: float32 [131072, 64], P(('grp', 'feat')), may hold values from -3 to 3
- frequencies: bfloat16 [32, 16384], P(None, 'feat'), may hold values from -1.5 to 1.5
- phases: float32 [16384], P('feat'), may hold values from 0 to 6.2832
- prior_weights: bfloat16 [16384, 64], P('feat'), may hold values from -6 to 6
- batch_tiles: int32 [2, 16, 1], P(None, 'grp'), may hold values from 0 to 63, as said below
Outputs:
- new_duals: float32 [131072, 64], P(('grp', 'feat'))
- new_velocity: float32 [131072, 64], P(('grp', 'feat'))
The draws below stay inside these ranges and needn't reach their ends.
Inputs may be any that keep to these rules, and one draw needn't show every extreme that they name: `batch_tiles`: in each step the 1 tile numbers of a group are distinct.
All inputs are finite; a program needn't handle non-finite values.
Results may differ from the reference program's by a relative error of at most 0.0012.
Values may be sent and summed in bfloat16 or wider, within the bound.
A program may use at most 64 MiB of HBM per device.

```python
import math
import jax
import jax.numpy as jnp
from jax import lax

D = 32
RFF = 16384
SAMPLES = 64
NPT = 256
TILE = 128
TILES_G = 1
STEPS = 2
GROUP_PTS = 8192
GROUP_TILES = 64
POINTS = 131072
BATCH = 2048
N_GRP = 16
DEVICES = 512


def place_value(chosen_row, slot_index, target_value):
    where_at = jnp.argmax(chosen_row == target_value)
    other_value = chosen_row[slot_index]
    return chosen_row.at[where_at].set(other_value).at[slot_index].set(target_value)


def draw_batch_tiles(key, part):
    group_total = BATCH // (TILES_G * TILE)
    subkeys = jax.random.split(key, STEPS * group_total)
    shuffled = jax.vmap(lambda subkey: jax.random.permutation(subkey, GROUP_TILES))(subkeys).astype(jnp.int32)
    first_group = jax.random.randint(jax.random.fold_in(key, 11), (), 0, group_total)
    first_slot = jax.random.randint(jax.random.fold_in(key, 12), (), 0, TILES_G)
    second_group = jax.random.randint(jax.random.fold_in(key, 13), (), 0, group_total) + group_total * (STEPS - 1)
    second_slot = jax.random.randint(jax.random.fold_in(key, 14), (), 0, TILES_G)
    shuffled = shuffled.at[first_group].set(place_value(shuffled[first_group], first_slot, GROUP_TILES - 1))
    shuffled = shuffled.at[second_group].set(place_value(shuffled[second_group], second_slot, 0))
    return shuffled[:, :TILES_G].reshape(STEPS, group_total, TILES_G).astype(jnp.int32)


def draw_points(key, part):
    label_key = jax.random.fold_in(key, 21)
    center_key = jax.random.fold_in(key, 22)
    spread_key = jax.random.fold_in(key, 23)
    labels = jax.random.randint(label_key, (POINTS,), 0, 4).astype(jnp.int32)
    centers = 1.1 * jax.random.normal(center_key, (4, D), jnp.float32)
    spread = 0.8 * jax.random.normal(spread_key, (POINTS, D), jnp.float32)
    values = jnp.clip(centers[labels] + spread, -6.0, 6.0)
    return values.astype(jnp.bfloat16)


def levels(own_key, extent, pieces, least, largest):
    factor_of = 1.0
    for position, blocks in pieces:
        steps = jax.random.uniform(jax.random.fold_in(jax.random.fold_in(own_key, 6), position), (blocks,), jnp.float32, least / len(pieces), largest / len(pieces))
        factor_of = factor_of * jnp.repeat(jnp.exp(steps), extent[position] // blocks).reshape((-1,) + (1,) * (len(extent) - 1 - position))
    return factor_of


def centred(key, dims, deviation, reach, cuts=(), kind=jnp.bfloat16):
    values = jax.random.normal(key, dims, jnp.float32) * deviation
    if len(cuts) > 0:
        values = levels(key, dims, cuts, -0.22, 0.18) * values
    return jnp.clip(values, min=-reach, max=reach).astype(kind)


def setup_inputs(seed: int = 0) -> dict:
    key_of = jax.random.split(jax.random.key(seed), 10)
    points = draw_points(jax.random.fold_in(key_of[9], 71), 0)
    dual_weights = centred(key_of[1], (POINTS, SAMPLES), 1.0, 6.0, ((0, 512),), jnp.float32)
    velocity = centred(key_of[2], (POINTS, SAMPLES), 0.3, 1.75, ((0, 512),), jnp.float32)
    observed = centred(key_of[3], (POINTS,), 2.0, 12.0, ((0, 512),), jnp.float32)
    noise_draws = centred(key_of[4], (POINTS, SAMPLES), 0.5, 3.0, ((0, 512),), jnp.float32)
    frequencies = centred(key_of[5], (D, RFF), ((2 / D) ** 0.5), 1.5, ((1, 32),))
    phases = jnp.clip(6.2832 * jax.random.uniform(key_of[6], (RFF,), jnp.float32) ** levels(key_of[6], (RFF,), ((0, 32),), -0.2, 0.2), 0.0, 6.2832)
    prior_weights = centred(key_of[7], (RFF, SAMPLES), 1.0, 6.0, ((0, 32),))
    batch_tiles = draw_batch_tiles(jax.random.fold_in(key_of[9], 71), 0)
    return {"points": points, "dual_weights": dual_weights, "velocity": velocity, "observed": observed, "noise_draws": noise_draws, "frequencies": frequencies, "phases": phases, "prior_weights": prior_weights, "batch_tiles": batch_tiles}


amplitude = 4.0
signal = 2.0
momentum = 0.9
step_size = 0.5

def kernel_values(picked, point_block, norm_block):
    row_sq = lax.optimization_barrier(jnp.sum(jnp.square(picked.astype(jnp.float32)), axis=1))
    inner_prod = lax.dot_general(picked, point_block, (((1,), (1,)), ((), ())), preferred_element_type=jnp.float32)
    distance = row_sq[:, None] + norm_block[None, :] - 2.0 * inner_prod
    return (amplitude * jnp.exp(-distance / point_block.shape[1])).astype(jnp.bfloat16)

def reference(points, dual_weights, velocity, observed, noise_draws, frequencies, phases, prior_weights, batch_tiles):
    inv_root = 1.0 / math.sqrt(POINTS)
    prior_scale = signal * math.sqrt(2.0 / RFF)
    norm_all = lax.optimization_barrier(jnp.sum(jnp.square(points.astype(jnp.float32)), axis=1))
    point_blocks = points.reshape(DEVICES, NPT, D)
    norm_blocks = norm_all.reshape(DEVICES, NPT)
    for step_index in range(STEPS):
        tile_ids = batch_tiles[step_index]
        row_ids = (jnp.arange(N_GRP, dtype=jnp.int32)[:, None, None] * GROUP_PTS + tile_ids[:, :, None] * TILE + jnp.arange(TILE, dtype=jnp.int32)[None, None, :]).reshape(-1).astype(jnp.int32)
        picked = points[row_ids]
        duals_bf = dual_weights.astype(jnp.bfloat16).reshape(DEVICES, NPT, SAMPLES)

        def add_block(running, block):
            point_block, norm_block, dual_block = block
            kernel_tile = kernel_values(picked, point_block, norm_block)
            return (running + jnp.dot(kernel_tile, dual_block, preferred_element_type=jnp.float32), None)
        summed, _ = lax.scan(add_block, jnp.zeros((BATCH, SAMPLES), jnp.float32), (point_blocks, norm_blocks, duals_bf))
        phase_arg = jnp.dot(picked, frequencies, preferred_element_type=jnp.float32) + phases[None, :]
        features = jnp.cos(phase_arg).astype(jnp.bfloat16)
        prior_vals = jnp.dot(features, prior_weights, preferred_element_type=jnp.float32) * prior_scale
        gradient = summed * inv_root + prior_vals - observed[row_ids][:, None] + noise_draws[row_ids]
        new_vel = momentum * velocity[row_ids] - step_size * gradient
        new_duals = dual_weights[row_ids] + new_vel
        dual_weights = dual_weights.at[row_ids].set(new_duals)
        velocity = velocity.at[row_ids].set(new_vel)
    return (dual_weights, velocity)
```

```python
import functools
import math

import jax
import jax.numpy as jnp
from jax import lax
from jax.experimental import pallas as pl
from jax.experimental.pallas import tpu as pltpu
from jax.sharding import PartitionSpec as P

TILE = 128
STEPS = 2
NX = 4
MESH = pl.DeviceIdType.MESH

amplitude = 4.0
signal = 2.0
momentum = 0.9
step_size = 0.5

F32 = jnp.float32
BF16 = jnp.bfloat16

PI_HI = 3.140625
PI_LO = 9.67653589793e-4
INV_TWO_PI = 0.15915494309189535


def cosine(arg):
    turns = jnp.floor(arg * INV_TWO_PI + 0.5)
    half = arg * 0.5 - turns * PI_HI
    half = half - turns * PI_LO
    sq = half * half
    poly = sq * 2.6000493542416553e-06 + -0.00019806612414667135
    poly = poly * sq + 0.0083330172462401
    poly = poly * sq + -0.16666657094222279
    sine = half + half * (sq * poly)
    return 1.0 - 2.0 * (sine * sine)


def dot00(a, b):
    return lax.dot_general(a, b, (((0,), (0,)), ((), ())), preferred_element_type=F32)


def dot11(a, b):
    return lax.dot_general(a, b, (((1,), (1,)), ((), ())), preferred_element_type=F32)


def dot10(a, b):
    return lax.dot_general(a, b, (((1,), (0,)), ((), ())), preferred_element_type=F32)


def split_norm(cols):
    wide = cols.astype(F32)
    norm = jnp.sum(wide * wide, axis=0, keepdims=True) * (-1.0 / cols.shape[0])
    hi = norm.astype(BF16).astype(F32)
    rest = norm - hi
    mid = rest.astype(BF16).astype(F32)
    return hi, mid, rest - mid


def extra_rows(terms, width, first):
    rows = lax.broadcasted_iota(jnp.int32, (16, width), 0)
    out = jnp.where((rows >= 3 - first) & (rows < 6 - first), 1.0, 0.0)
    for i in range(3):
        out = jnp.where(rows == first + i, terms[i], out)
    return out.astype(BF16)


def kernel(
    nx, ny, nz, total_points, total_feats,
    bt, pT, uT, vT, ob, nT, fr, ph, wT,
    ou, ov,
    gat, pa, xs1, xr1, xs2, xr2, xa, xy, pa0, kc,
    pf, pr, zs, zr, vg, vy, cs, co, fin, cr, ssem, rsem,
):
    nh = nz // 2
    ns = nx * 2
    g = lax.axis_index("grp")
    f = lax.axis_index("feat")
    y = lax.div(g, 2)
    zl = lax.rem(g, 2)
    x = lax.div(f, nh * 2)
    c = lax.rem(f, 2)
    zh = lax.rem(lax.div(f, 2), nh)
    z = zh * 2 + zl
    s = x * 2 + c

    def at(s_, y_, z_):
        return {
            "grp": y_ * 2 + lax.rem(z_, 2),
            "feat": lax.div(s_, 2) * (nh * 2) + lax.div(z_, 2) * 2 + lax.rem(s_, 2),
        }

    def far_first(n):
        return sorted(range(1, n), key=lambda k: -min(k, n - k))

    block_of = {j: lax.rem(s + j, ns) for j in range(1, ns)}
    s_order = sorted(range(1, ns), key=lambda j: (-min(j, ns - j), j))
    z_flip = zh * 2 + (1 - zl)
    s_dev = {j: at(block_of[j], y, z) for j in block_of}
    p_dev = {j: at(block_of[j], y, z_flip) for j in block_of}
    p_dev[0] = at(s, y, z_flip)
    y_dev = {k: at(s, lax.rem(y + k, ny), z) for k in range(1, ny)}
    z_dev = {k: at(s, y, lax.rem(z + k, nz)) for k in range(1, nz)}

    barrier = pltpu.get_barrier_semaphore()
    greeted = list(s_dev.values()) + list(y_dev.values()) + list(z_dev.values())
    greeted += [p_dev[j] for j in block_of]
    for d in greeted:
        pl.semaphore_signal(barrier, inc=1, device_id=d, device_id_type=MESH)

    started = []

    def send(src, dst, dev):
        i = len(started)
        copy = pltpu.make_async_remote_copy(
            src_ref=src, dst_ref=dst, send_sem=ssem.at[i], recv_sem=rsem.at[i],
            device_id=dev, device_id_type=MESH,
        )
        copy.start()
        started.append(copy)
        return copy

    def owned(t):
        tile = bt[t]
        return lax.div(tile, 2) == f, lax.rem(tile, 2) == 0

    def pick(ref, low):
        return jnp.where(low, ref[:, :TILE], ref[:, TILE:])

    gat[0, 0:32, :] = pT[...]
    gat[0, 32:96, :] = uT[...].astype(BF16)
    for t in range(STEPS):
        mine, low = owned(t)
        xs1[t] = jnp.where(mine, pick(pT, low).astype(F32), 0.0).astype(BF16)
    pl.semaphore_wait(barrier, len(greeted))

    hop_c = [[send(xs1.at[t], xr1.at[j, t], s_dev[j]) for j in s_order] for t in range(STEPS)]
    bulk = {k: send(gat.at[0], gat.at[k], y_dev[k]) for k in far_first(ny)}
    hop_d = []
    for t in range(STEPS):
        for copy in hop_c[t]:
            copy.wait_recv()
        acc = xs1[t]
        for j in range(1, ns):
            acc = acc + xr1[j, t]
        xs2[t] = acc
        hop_d.append([send(xs2.at[t], xr2.at[k, t], z_dev[k]) for k in far_first(nz)])

    def build_points(k):
        block = gat[k, 0:32, :]
        pa[k, 0:32, :] = block
        pa[k, 32:48, :] = extra_rows(split_norm(block), 2 * TILE, 3)

    def batch_rows(t):
        for copy in hop_d[t]:
            copy.wait_recv()
        own = xs2[t]
        for k in range(2, nz, 2):
            own = own + xr2[k, t]
        oth = xr2[1, t]
        for k in range(3, nz, 2):
            oth = oth + xr2[k, t]
        if t == 0:
            xy[0] = own
        for i, rows in enumerate((own, oth)):
            lanes = slice(i * TILE, (i + 1) * TILE)
            xa[t, 0:32, lanes] = (rows.astype(F32) * (2.0 / 32)).astype(BF16)
            xa[t, 32:48, lanes] = extra_rows(split_norm(rows), TILE, 0)
        return own

    kv_scale = -step_size * amplitude / math.sqrt(total_points)
    prior_scale = -step_size * signal * math.sqrt(2.0 / total_feats)

    def prior_part(rows):
        feats = cosine(dot00(rows, fr[...]) + ph[...]).astype(BF16)
        return dot11(wT[...], feats) * prior_scale

    def kernel_part(t):
        xat = xa[t]

        def one(k, acc):
            kern = jnp.exp(dot00(pa[k], xat)).astype(BF16)
            return acc + dot10(gat[k, 32:96, :], kern)

        return lax.fori_loop(0, ny, one, jnp.zeros((64, 2 * TILE), F32), unroll=True) * kv_scale

    def own_terms(t):
        mine, low = owned(t)
        terms = step_size * (pick(ob, low) - pick(nT, low))
        if t == 0:
            terms = terms + momentum * pick(vT, low)
        return jnp.where(mine, terms, 0.0)

    def partial(t, prior):
        part = kernel_part(t)
        own = part[:, :TILE] + prior + own_terms(t)
        pf[t, :, :, 0:TILE] = own.reshape(ns, 64 // ns, TILE)
        pf[t, :, :, TILE:] = part[:, TILE:].reshape(ns, 64 // ns, TILE)
        return [send(pf.at[t, block_of[j]], pr.at[t, j], s_dev[j]) for j in s_order]

    def stage_z(t, hops):
        for copy in hops:
            copy.wait_recv()
        share = pf[t, s]
        for j in range(1, ns):
            share = share + pr[t, j]
        zs[t, 0] = share[:, :TILE]
        zs[t, 1] = share[:, TILE:]
        return [send(zs.at[t, k % 2], zr.at[t, k], z_dev[k]) for k in far_first(nz)]

    def stage_end(t, hops):
        for copy in hops:
            copy.wait_recv()
        share = zs[t, 0]
        for k in range(1, nz):
            share = share + zr[t, k]
        return share

    build_points(0)
    rows0 = batch_rows(0)
    hop_xy = [send(xy.at[0], xy.at[k], y_dev[k]) for k in far_first(ny)]
    prior0 = prior_part(rows0)
    for k in far_first(ny):
        bulk[k].wait_recv()
        build_points(k)
    hops0 = partial(0, prior0)
    rows1 = batch_rows(1)
    hops0 = stage_z(0, hops0)
    hops1 = partial(1, prior_part(rows1))
    vel0 = stage_end(0, hops0)
    vy[0] = vel0
    hop_vy = {k: send(vy.at[0], vy.at[k], y_dev[k]) for k in far_first(ny)}
    vg[s] = vel0
    hop_g = [send(vy.at[0], vg.at[s], s_dev[j]) for j in s_order]
    hops1 = stage_z(1, hops1)
    for copy in hop_xy:
        copy.wait_recv()
    xa1 = xa[1]
    for k in range(ny):
        block = xy[k]
        pa0[k, 0:32, :] = block
        pa0[k, 32:48, :] = extra_rows(split_norm(block), TILE, 3)
        kc[k] = jnp.exp(dot00(pa0[k], xa1)).astype(BF16)
    for copy in hop_g:
        copy.wait_recv()
    new0 = vg[...].reshape(64, TILE)
    mine, low = owned(0)
    for h in range(2):
        lanes = slice(h * TILE, (h + 1) * TILE)
        here = mine & (low == (h == 0))
        ov[:, lanes] = jnp.where(here, new0, vT[:, lanes])
        ou[:, lanes] = jnp.where(here, uT[:, lanes] + new0, uT[:, lanes])
    base1 = stage_end(1, hops1)

    corr = dot10(vy[0].astype(BF16), kc[0])
    for k in far_first(ny):
        hop_vy[k].wait_recv()
        corr = corr + dot10(vy[k].astype(BF16), kc[k])
    corr = corr * kv_scale
    cs[...] = corr[:, :TILE] + base1
    co[...] = corr[:, TILE:]
    fin[s] = cs[...]
    last = [send(co, cr.at[s], p_dev[j]) for j in s_order + [0]]
    last += [send(cs, fin.at[s], s_dev[j]) for j in s_order]
    for copy in last:
        copy.wait_recv()
    mine, low = owned(1)
    new1 = (fin[...] + cr[...]).reshape(64, TILE) + momentum * pick(ov, low)
    for h in range(2):
        lanes = slice(h * TILE, (h + 1) * TILE)
        here = mine & (low == (h == 0))
        before_v = ov[:, lanes]
        before_u = ou[:, lanes]
        ov[:, lanes] = jnp.where(here, new1, before_v)
        ou[:, lanes] = jnp.where(here, before_u + new1, before_u)
    for copy in started:
        copy.wait_send()


def local(
    nx, ny, nz,
    points, dual_weights, velocity, observed, noise_draws, frequencies, phases,
    prior_weights, batch_tiles,
):
    own, samples = dual_weights.shape
    feats = phases.shape[0]
    ns = nx * 2
    copies = 3 * (ny - 1) + 7 * (ns - 1) + 1 + 4 * (nz - 1)
    vm = pltpu.VMEM
    share = samples // ns
    out = jax.ShapeDtypeStruct((samples, own), F32)
    new_u, new_v = pl.pallas_call(
        functools.partial(
            kernel, nx, ny, nz, own * nx * ny * nz * 2, feats * nx * nz
        ),
        out_shape=(out, out),
        in_specs=[pl.BlockSpec(memory_space=pltpu.SMEM)]
        + [pl.BlockSpec(memory_space=pltpu.VMEM)] * 8,
        out_specs=(pl.BlockSpec(memory_space=pltpu.VMEM),) * 2,
        scratch_shapes=[
            vm((ny, 32 + samples, own), BF16),
            vm((ny, 48, own), BF16),
            vm((STEPS, 32, TILE), BF16),
            vm((ns, STEPS, 32, TILE), BF16),
            vm((STEPS, 32, TILE), BF16),
            vm((nz, STEPS, 32, TILE), BF16),
            vm((STEPS, 48, 2 * TILE), BF16),
            vm((ny, 32, TILE), BF16),
            vm((ny, 48, TILE), BF16),
            vm((ny, TILE, 2 * TILE), BF16),
            vm((STEPS, ns, share, 2 * TILE), F32),
            vm((STEPS, ns, share, 2 * TILE), F32),
            vm((STEPS, 2, share, TILE), F32),
            vm((STEPS, nz, share, TILE), F32),
            vm((ns, share, TILE), F32),
            vm((ny, share, TILE), F32),
            vm((share, TILE), F32),
            vm((share, TILE), F32),
            vm((ns, share, TILE), F32),
            vm((ns, share, TILE), F32),
            pltpu.SemaphoreType.DMA((copies,)),
            pltpu.SemaphoreType.DMA((copies,)),
        ],
        compiler_params=pltpu.CompilerParams(collective_id=0, has_side_effects=True),
    )(
        batch_tiles.reshape(STEPS),
        points.T,
        dual_weights.T,
        velocity.T,
        observed.reshape(1, own),
        noise_draws.T,
        frequencies,
        phases.reshape(1, feats),
        prior_weights.T,
    )
    return new_u.T, new_v.T


def solution(mesh):
    nx = NX
    ny = mesh.shape["grp"] // 2
    nz = mesh.shape["feat"] // nx
    return jax.shard_map(
        functools.partial(local, nx, ny, nz),
        mesh=mesh,
        in_specs=(
            P(("grp", "feat"), None),
            P(("grp", "feat"), None),
            P(("grp", "feat"), None),
            P(("grp", "feat")),
            P(("grp", "feat"), None),
            P(None, "feat"),
            P("feat"),
            P("feat", None),
            P(None, "grp", None),
        ),
        out_specs=(P(("grp", "feat"), None), P(("grp", "feat"), None)),
        check_vma=False,
    )
```

```python
import functools
import math

import jax
import jax.numpy as jnp
from jax import lax
from jax.experimental import pallas as pl
from jax.experimental.pallas import tpu as pltpu
from jax.sharding import PartitionSpec as P

TILE = 128
STEPS = 2
NX = 4
MESH = pl.DeviceIdType.MESH

amplitude = 4.0
signal = 2.0
momentum = 0.9
step_size = 0.5

F32 = jnp.float32
BF16 = jnp.bfloat16

PI_HI = 3.140625
PI_LO = 9.67653589793e-4
INV_TWO_PI = 0.15915494309189535


def cosine(arg):
    turns = jnp.floor(arg * INV_TWO_PI + 0.5)
    half = arg * 0.5 - turns * PI_HI
    half = half - turns * PI_LO
    sq = half * half
    poly = sq * 2.6000493542416553e-06 + -0.00019806612414667135
    poly = poly * sq + 0.0083330172462401
    poly = poly * sq + -0.16666657094222279
    sine = half + half * (sq * poly)
    return 1.0 - 2.0 * (sine * sine)


def dot00(a, b):
    return lax.dot_general(a, b, (((0,), (0,)), ((), ())), preferred_element_type=F32)


def dot11(a, b):
    return lax.dot_general(a, b, (((1,), (1,)), ((), ())), preferred_element_type=F32)


def dot10(a, b):
    return lax.dot_general(a, b, (((1,), (0,)), ((), ())), preferred_element_type=F32)


def split_norm(cols):
    wide = cols.astype(F32)
    norm = jnp.sum(wide * wide, axis=0, keepdims=True) * (-1.0 / cols.shape[0])
    hi = norm.astype(BF16).astype(F32)
    rest = norm - hi
    mid = rest.astype(BF16).astype(F32)
    return hi, mid, rest - mid


def extra_rows(terms, width, first):
    rows = lax.broadcasted_iota(jnp.int32, (16, width), 0)
    out = jnp.where((rows >= 3 - first) & (rows < 6 - first), 1.0, 0.0)
    for i in range(3):
        out = jnp.where(rows == first + i, terms[i], out)
    return out.astype(BF16)


def kernel(
    nx, ny, nz, total_points, total_feats,
    bt_in, pT_in, uT_in, vT_in, ob_in, nT_in, fr_in, ph_in, wT_in,
    du, dv,
    bt, uT, vT, ob, nT, fr, ph, wT,
    gat, pa, xs1, xr1, xs2, xr2, xa, xy, pa0, kc,
    pf, pr, zs, zr, vg, vy, cs, co, fin, cr, isem, ssem, rsem,
):
    nh = nz // 2
    ns = nx * 2
    loads = []
    for i, (src, dst) in enumerate((
        (bt_in, bt), (pT_in, gat.at[0, pl.ds(0, 32)]), (uT_in, uT), (fr_in, fr), (ph_in, ph),
        (wT_in, wT), (ob_in, ob), (nT_in, nT), (vT_in, vT),
    )):
        loads.append(pltpu.make_async_copy(src, dst, isem.at[i]))
        loads[-1].start()

    g = lax.axis_index("grp")
    f = lax.axis_index("feat")
    y = lax.div(g, 2)
    zl = lax.rem(g, 2)
    x = lax.div(f, nh * 2)
    c = lax.rem(f, 2)
    zh = lax.rem(lax.div(f, 2), nh)
    z = zh * 2 + zl
    s = x * 2 + c

    def at(s_, y_, z_):
        return {
            "grp": y_ * 2 + lax.rem(z_, 2),
            "feat": lax.div(s_, 2) * (nh * 2) + lax.div(z_, 2) * 2 + lax.rem(s_, 2),
        }

    def far_first(n):
        return sorted(range(1, n), key=lambda k: -min(k, n - k))

    block_of = {j: lax.rem(s + j, ns) for j in range(1, ns)}
    s_order = sorted(range(1, ns), key=lambda j: (-min(j, ns - j), j))
    z_flip = zh * 2 + (1 - zl)
    s_dev = {j: at(block_of[j], y, z) for j in block_of}
    p_dev = {j: at(block_of[j], y, z_flip) for j in block_of}
    p_dev[0] = at(s, y, z_flip)
    y_dev = {k: at(s, lax.rem(y + k, ny), z) for k in range(1, ny)}
    z_dev = {k: at(s, y, lax.rem(z + k, nz)) for k in range(1, nz)}

    barrier = pltpu.get_barrier_semaphore()
    greeted = [z_dev[k] for k in far_first(nz)] + [y_dev[k] for k in far_first(ny)]
    greeted += [p_dev[j] for j in s_order] + [s_dev[j] for j in s_order]
    for d in greeted:
        pl.semaphore_signal(barrier, inc=1, device_id=d, device_id_type=MESH)

    counts = [0, 0]
    closing = []

    def stage(copies, landing):
        i = counts[0]
        counts[0] += 1
        for src, dst, dev in copies:
            pltpu.make_async_remote_copy(
                src_ref=src, dst_ref=dst, send_sem=ssem.at[i], recv_sem=rsem.at[i],
                device_id=dev, device_id_type=MESH,
            ).start()
        whole = pltpu.make_async_remote_copy(
            src_ref=landing, dst_ref=landing, send_sem=ssem.at[i], recv_sem=rsem.at[i],
            device_id=copies[0][2], device_id_type=MESH,
        )
        closing.append(whole)
        return whole

    def owned(t):
        tile = bt[t]
        return lax.div(tile, 2) == f, lax.rem(tile, 2) == 0

    def pick(ref, low):
        return jnp.where(low, ref[:, :TILE], ref[:, TILE:])

    loads[0].wait()
    loads[1].wait()
    for t in range(STEPS):
        mine, low = owned(t)
        tile_rows = jnp.where(low, gat[0, 0:32, 0:TILE], gat[0, 0:32, TILE:])
        xs1[t] = jnp.where(mine, tile_rows.astype(F32), 0.0).astype(BF16)
    pl.semaphore_wait(barrier, len(greeted))

    hop_c = [
        stage([(xs1.at[t], xr1.at[t, j], s_dev[j]) for j in s_order], xr1.at[t, pl.ds(1, ns - 1)])
        for t in range(STEPS)
    ]
    loads[2].wait()
    gat[0, 32:96, :] = uT[...].astype(BF16)
    bulk = stage([(gat.at[0], gat.at[k], y_dev[k]) for k in far_first(ny)], gat.at[pl.ds(1, ny - 1)])
    hop_d = []
    for t in range(STEPS):
        hop_c[t].wait_recv()
        acc = xs1[t]
        for j in range(1, ns):
            acc = acc + xr1[t, j]
        xs2[t] = acc
        hop_d.append(stage(
            [(xs2.at[t], xr2.at[t, k], z_dev[k]) for k in far_first(nz)], xr2.at[t, pl.ds(1, nz - 1)]
        ))
    for load in loads[3:]:
        load.wait()

    def build_points(k):
        block = gat[k, 0:32, :]
        pa[k, 0:32, :] = block
        pa[k, 32:48, :] = extra_rows(split_norm(block), 2 * TILE, 3)

    def batch_rows(t):
        hop_d[t].wait_recv()
        own = xs2[t]
        for k in range(2, nz, 2):
            own = own + xr2[t, k]
        oth = xr2[t, 1]
        for k in range(3, nz, 2):
            oth = oth + xr2[t, k]
        if t == 0:
            xy[0] = own
        for i, rows in enumerate((own, oth)):
            lanes = slice(i * TILE, (i + 1) * TILE)
            xa[t, 0:32, lanes] = (rows.astype(F32) * (2.0 / 32)).astype(BF16)
            xa[t, 32:48, lanes] = extra_rows(split_norm(rows), TILE, 0)
        return own

    kv_scale = -step_size * amplitude / math.sqrt(total_points)
    prior_scale = -step_size * signal * math.sqrt(2.0 / total_feats)

    def prior_part(rows):
        feats = cosine(dot00(rows, fr[...]) + ph[...]).astype(BF16)
        return dot11(wT[...], feats) * prior_scale

    def kernel_part(t):
        xat = xa[t]

        def one(k, acc):
            kern = jnp.exp(dot00(pa[k], xat)).astype(BF16)
            return acc + dot10(gat[k, 32:96, :], kern)

        return lax.fori_loop(0, ny, one, jnp.zeros((64, 2 * TILE), F32), unroll=True) * kv_scale

    def own_terms(t):
        mine, low = owned(t)
        terms = step_size * (pick(ob, low) - pick(nT, low))
        if t == 0:
            terms = terms + momentum * pick(vT, low)
        return jnp.where(mine, terms, 0.0)

    def partial(t, prior):
        part = kernel_part(t)
        own = part[:, :TILE] + prior
        pf[t, :, :, 0:TILE] = own.reshape(ns, 64 // ns, TILE)
        pf[t, :, :, TILE:] = part[:, TILE:].reshape(ns, 64 // ns, TILE)
        return stage(
            [(pf.at[t, block_of[j]], pr.at[t, j], s_dev[j]) for j in s_order],
            pr.at[t, pl.ds(1, ns - 1)],
        )

    def stage_z(t, hop):
        hop.wait_recv()
        share = pf[t, s]
        for j in range(1, ns):
            share = share + pr[t, j]
        zs[t, 0] = share[:, :TILE]
        zs[t, 1] = share[:, TILE:]
        return stage(
            [(zs.at[t, k % 2], zr.at[t, k], z_dev[k]) for k in far_first(nz)],
            zr.at[t, pl.ds(1, nz - 1)],
        )

    def stage_end(t, hop):
        hop.wait_recv()
        share = zs[t, 0]
        for k in range(1, nz):
            share = share + zr[t, k]
        return share

    build_points(0)
    base0 = own_terms(0)
    rows0 = batch_rows(0)
    hop_xy = stage([(xy.at[0], xy.at[k], y_dev[k]) for k in far_first(ny)], xy.at[pl.ds(1, ny - 1)])
    prior0 = prior_part(rows0) + base0
    bulk.wait_recv()
    for k in range(1, ny):
        build_points(k)
    hop0 = partial(0, prior0)
    base1 = own_terms(1)
    rows1 = batch_rows(1)
    hop0 = stage_z(0, hop0)
    hop1 = partial(1, prior_part(rows1) + base1)
    vel0 = stage_end(0, hop0)
    vy[0] = vel0
    hop_vy = stage([(vy.at[0], vy.at[k], y_dev[k]) for k in far_first(ny)], vy.at[pl.ds(1, ny - 1)])
    vg[s] = vel0
    hop_g = stage([(vy.at[0], vg.at[s], s_dev[j]) for j in s_order], vg.at[pl.ds(1, ns - 1)])
    hop1 = stage_z(1, hop1)
    hop_xy.wait_recv()
    xa1 = xa[1]
    for k in range(ny):
        block = xy[k]
        pa0[k, 0:32, :] = block
        pa0[k, 32:48, :] = extra_rows(split_norm(block), TILE, 3)
        kc[k] = jnp.exp(dot00(pa0[k], xa1)).astype(BF16)
    hop_g.wait_recv()
    new0 = vg[...].reshape(64, TILE)
    mine, low = owned(0)
    for h in range(2):
        lanes = slice(h * TILE, (h + 1) * TILE)
        here = mine & (low == (h == 0))
        du[:, lanes] = jnp.where(here, new0, 0.0)
        dv[:, lanes] = jnp.where(here, new0 - vT[:, lanes], 0.0)
    share1 = stage_end(1, hop1)
    mine, low = owned(1)
    kept = momentum * (pick(vT, low) + pick(dv, low))

    hop_vy.wait_recv()
    corr = dot10(vy[0].astype(BF16), kc[0])
    for k in range(1, ny):
        corr = corr + dot10(vy[k].astype(BF16), kc[k])
    corr = corr * kv_scale
    cs[...] = corr[:, :TILE] + share1
    co[...] = corr[:, TILE:]
    fin[s] = cs[...]
    last = stage([(co, cr.at[s], p_dev[j]) for j in s_order + [0]], cr)
    last_s = stage([(cs, fin.at[s], s_dev[j]) for j in s_order], fin.at[pl.ds(1, ns - 1)])
    for whole in closing[:-2]:
        whole.wait_send()
    last.wait_recv()
    last_s.wait_recv()
    new1 = (fin[...] + cr[...]).reshape(64, TILE) + kept
    for h in range(2):
        lanes = slice(h * TILE, (h + 1) * TILE)
        here = mine & (low == (h == 0))
        du[:, lanes] = du[:, lanes] + jnp.where(here, new1, 0.0)
        dv[:, lanes] = jnp.where(here, new1 - vT[:, lanes], dv[:, lanes])
    last.wait_send()
    last_s.wait_send()


def local(
    nx, ny, nz,
    points, dual_weights, velocity, observed, noise_draws, frequencies, phases,
    prior_weights, batch_tiles,
):
    own, samples = dual_weights.shape
    feats = phases.shape[0]
    ns = nx * 2
    stages = 14
    vm = pltpu.VMEM
    share = samples // ns
    out = jax.ShapeDtypeStruct((samples, own), F32)
    add_u, add_v = pl.pallas_call(
        functools.partial(
            kernel, nx, ny, nz, own * nx * ny * nz * 2, feats * nx * nz
        ),
        out_shape=(out, out),
        in_specs=[pl.BlockSpec(memory_space=pl.ANY)] * 9,
        out_specs=(pl.BlockSpec(memory_space=pltpu.VMEM),) * 2,
        scratch_shapes=[
            pltpu.SMEM((STEPS,), jnp.int32),
            vm((samples, own), F32),
            vm((samples, own), F32),
            vm((1, own), F32),
            vm((samples, own), F32),
            vm((32, feats), BF16),
            vm((1, feats), F32),
            vm((samples, feats), BF16),
            vm((ny, 32 + samples, own), BF16),
            vm((ny, 48, own), BF16),
            vm((STEPS, 32, TILE), BF16),
            vm((STEPS, ns, 32, TILE), BF16),
            vm((STEPS, 32, TILE), BF16),
            vm((STEPS, nz, 32, TILE), BF16),
            vm((STEPS, 48, 2 * TILE), BF16),
            vm((ny, 32, TILE), BF16),
            vm((ny, 48, TILE), BF16),
            vm((ny, TILE, 2 * TILE), BF16),
            vm((STEPS, ns, share, 2 * TILE), F32),
            vm((STEPS, ns, share, 2 * TILE), F32),
            vm((STEPS, 2, share, TILE), F32),
            vm((STEPS, nz, share, TILE), F32),
            vm((ns, share, TILE), F32),
            vm((ny, share, TILE), F32),
            vm((share, TILE), F32),
            vm((share, TILE), F32),
            vm((ns, share, TILE), F32),
            vm((ns, share, TILE), F32),
            pltpu.SemaphoreType.DMA((9,)),
            pltpu.SemaphoreType.DMA((stages,)),
            pltpu.SemaphoreType.DMA((stages,)),
        ],
        compiler_params=pltpu.CompilerParams(collective_id=0, has_side_effects=True),
    )(
        batch_tiles.reshape(STEPS),
        points.T,
        dual_weights.T,
        velocity.T,
        observed.reshape(1, own),
        noise_draws.T,
        frequencies,
        phases.reshape(1, feats),
        prior_weights.T,
    )
    return dual_weights + add_u.T, velocity + add_v.T


def solution(mesh):
    nx = NX
    ny = mesh.shape["grp"] // 2
    nz = mesh.shape["feat"] // nx
    return jax.shard_map(
        functools.partial(local, nx, ny, nz),
        mesh=mesh,
        in_specs=(
            P(("grp", "feat"), None),
            P(("grp", "feat"), None),
            P(("grp", "feat"), None),
            P(("grp", "feat")),
            P(("grp", "feat"), None),
            P(None, "feat"),
            P("feat"),
            P("feat", None),
            P(None, "grp", None),
        ),
        out_specs=(P(("grp", "feat"), None), P(("grp", "feat"), None)),
        check_vma=False,
    )
```

```python
import functools
import math

import jax
import jax.numpy as jnp
from jax import lax
from jax.experimental import pallas as pl
from jax.experimental.pallas import tpu as pltpu
from jax.sharding import PartitionSpec as P

TILE = 128
STEPS = 2
NX = 4
MESH = pl.DeviceIdType.MESH

amplitude = 4.0
signal = 2.0
momentum = 0.9
step_size = 0.5

F32 = jnp.float32
BF16 = jnp.bfloat16

PI_HI = 3.140625
PI_LO = 9.67653589793e-4
INV_TWO_PI = 0.15915494309189535


def cosine(arg):
    turns = jnp.floor(arg * INV_TWO_PI + 0.5)
    half = arg * 0.5 - turns * PI_HI
    half = half - turns * PI_LO
    sq = half * half
    poly = sq * 2.6000493542416553e-06 + -0.00019806612414667135
    poly = poly * sq + 0.0083330172462401
    poly = poly * sq + -0.16666657094222279
    sine = half + half * (sq * poly)
    return 1.0 - 2.0 * (sine * sine)


def dot00(a, b):
    return lax.dot_general(a, b, (((0,), (0,)), ((), ())), preferred_element_type=F32)


def dot11(a, b):
    return lax.dot_general(a, b, (((1,), (1,)), ((), ())), preferred_element_type=F32)


def dot10(a, b):
    return lax.dot_general(a, b, (((1,), (0,)), ((), ())), preferred_element_type=F32)


def split_norm(cols):
    wide = cols.astype(F32)
    norm = jnp.sum(wide * wide, axis=0, keepdims=True) * (-1.0 / cols.shape[0])
    hi = norm.astype(BF16).astype(F32)
    rest = norm - hi
    mid = rest.astype(BF16).astype(F32)
    return hi, mid, rest - mid


def extra_rows(terms, width, first):
    rows = lax.broadcasted_iota(jnp.int32, (16, width), 0)
    out = jnp.where((rows >= 3 - first) & (rows < 6 - first), 1.0, 0.0)
    for i in range(3):
        out = jnp.where(rows == first + i, terms[i], out)
    return out.astype(BF16)


def kernel(
    nx, ny, nz, total_points, total_feats,
    bt_in, pT_in, uT_in, vT_in, ob_in, nT_in, fr_in, ph_in, wT_in,
    du, dv,
    bt, uT, vT, ob, nT, fr, ph, wT,
    gat, pa, xs1, xr1, xs2, xr2, xa, xy, pa0, kc,
    pf, pr, zs, zr, vg, vy, cs, co, fin, cr, isem, ssem, rsem,
):
    nh = nz // 2
    ns = nx * 2
    loads = []
    for i, (src, dst) in enumerate((
        (bt_in, bt), (pT_in, gat.at[0, pl.ds(0, 32)]), (uT_in, uT), (fr_in, fr), (ph_in, ph),
        (wT_in, wT), (ob_in, ob), (nT_in, nT), (vT_in, vT),
    )):
        loads.append(pltpu.make_async_copy(src, dst, isem.at[i]))
        loads[-1].start()

    g = lax.axis_index("grp")
    f = lax.axis_index("feat")
    y = lax.div(g, 2)
    zl = lax.rem(g, 2)
    x = lax.div(f, nh * 2)
    c = lax.rem(f, 2)
    zh = lax.rem(lax.div(f, 2), nh)
    z = zh * 2 + zl
    s = x * 2 + c

    def at(s_, y_, z_):
        return {
            "grp": y_ * 2 + lax.rem(z_, 2),
            "feat": lax.div(s_, 2) * (nh * 2) + lax.div(z_, 2) * 2 + lax.rem(s_, 2),
        }

    def far_first(n):
        return sorted(range(1, n), key=lambda k: -min(k, n - k))

    block_of = {j: lax.rem(s + j, ns) for j in range(1, ns)}
    s_order = sorted(range(1, ns), key=lambda j: (-min(j, ns - j), j))
    z_flip = zh * 2 + (1 - zl)
    s_dev = {j: at(block_of[j], y, z) for j in block_of}
    p_dev = {j: at(block_of[j], y, z_flip) for j in block_of}
    p_dev[0] = at(s, y, z_flip)
    y_dev = {k: at(s, lax.rem(y + k, ny), z) for k in range(1, ny)}
    z_dev = {k: at(s, y, lax.rem(z + k, nz)) for k in range(1, nz)}

    barrier = pltpu.get_barrier_semaphore()
    greeted = [z_dev[k] for k in far_first(nz)] + [y_dev[k] for k in far_first(ny)]
    greeted += [p_dev[j] for j in s_order] + [s_dev[j] for j in s_order]
    for d in greeted:
        pl.semaphore_signal(barrier, inc=1, device_id=d, device_id_type=MESH)

    counts = [0, 0]
    closing = []

    def stage(copies, landing):
        i = counts[0]
        counts[0] += 1
        for src, dst, dev in copies:
            pltpu.make_async_remote_copy(
                src_ref=src, dst_ref=dst, send_sem=ssem.at[i], recv_sem=rsem.at[i],
                device_id=dev, device_id_type=MESH,
            ).start()
        whole = pltpu.make_async_remote_copy(
            src_ref=landing, dst_ref=landing, send_sem=ssem.at[i], recv_sem=rsem.at[i],
            device_id=copies[0][2], device_id_type=MESH,
        )
        closing.append(whole)
        return whole

    def owned(t):
        tile = bt[t]
        return lax.div(tile, 2) == f, lax.rem(tile, 2) == 0

    def pick(ref, low):
        return jnp.where(low, ref[:, :TILE], ref[:, TILE:])

    loads[0].wait()
    loads[1].wait()
    for t in range(STEPS):
        mine, low = owned(t)
        tile_rows = jnp.where(low, gat[0, 0:32, 0:TILE], gat[0, 0:32, TILE:])
        xs1[t] = jnp.where(mine, tile_rows.astype(F32), 0.0).astype(BF16)
    pl.semaphore_wait(barrier, len(greeted))

    hop_c = [
        stage([(xs1.at[t], xr1.at[t, j], s_dev[j]) for j in s_order], xr1.at[t, pl.ds(1, ns - 1)])
        for t in range(STEPS)
    ]
    loads[2].wait()
    gat[0, 32:96, :] = uT[...].astype(BF16)
    bulk = stage([(gat.at[0], gat.at[k], y_dev[k]) for k in far_first(ny)], gat.at[pl.ds(1, ny - 1)])
    hop_d = []
    for t in range(STEPS):
        hop_c[t].wait_recv()
        acc = xs1[t]
        for j in range(1, ns):
            acc = acc + xr1[t, j]
        xs2[t] = acc
        hop_d.append(stage(
            [(xs2.at[t], xr2.at[t, k], z_dev[k]) for k in far_first(nz)], xr2.at[t, pl.ds(1, nz - 1)]
        ))
    for load in loads[3:]:
        load.wait()

    def build_points(k):
        block = gat[k, 0:32, :]
        pa[k, 0:32, :] = block
        pa[k, 32:48, :] = extra_rows(split_norm(block), 2 * TILE, 3)

    def batch_rows(t):
        hop_d[t].wait_recv()
        own = xs2[t]
        for k in range(2, nz, 2):
            own = own + xr2[t, k]
        oth = xr2[t, 1]
        for k in range(3, nz, 2):
            oth = oth + xr2[t, k]
        if t == 0:
            xy[0] = own
        for i, rows in enumerate((own, oth)):
            lanes = slice(i * TILE, (i + 1) * TILE)
            xa[t, 0:32, lanes] = (rows.astype(F32) * (2.0 / 32)).astype(BF16)
            xa[t, 32:48, lanes] = extra_rows(split_norm(rows), TILE, 0)
        return own

    kv_scale = -step_size * amplitude / math.sqrt(total_points)
    prior_scale = -step_size * signal * math.sqrt(2.0 / total_feats)

    def prior_part(rows):
        feats = cosine(dot00(rows, fr[...]) + ph[...]).astype(BF16)
        return dot11(wT[...], feats) * prior_scale

    def kernel_part(t):
        xat = xa[t]

        def one(k, acc):
            kern = jnp.exp(dot00(pa[k], xat)).astype(BF16)
            return acc + dot10(gat[k, 32:96, :], kern)

        return lax.fori_loop(0, ny, one, jnp.zeros((64, 2 * TILE), F32), unroll=True) * kv_scale

    def own_terms(t):
        mine, low = owned(t)
        terms = step_size * (pick(ob, low) - pick(nT, low))
        if t == 0:
            terms = terms + momentum * pick(vT, low)
        return jnp.where(mine, terms, 0.0)

    def partial(t, prior):
        part = kernel_part(t)
        own = part[:, :TILE] + prior
        pf[t, :, :, 0:TILE] = own.reshape(ns, 64 // ns, TILE)
        pf[t, :, :, TILE:] = part[:, TILE:].reshape(ns, 64 // ns, TILE)
        return stage(
            [(pf.at[t, block_of[j]], pr.at[t, j], s_dev[j]) for j in s_order],
            pr.at[t, pl.ds(1, ns - 1)],
        )

    def stage_z(t, hop):
        hop.wait_recv()
        share = pf[t, s]
        for j in range(1, ns):
            share = share + pr[t, j]
        zs[t, 0] = share[:, :TILE]
        zs[t, 1] = share[:, TILE:]
        return stage(
            [(zs.at[t, k % 2], zr.at[t, k], z_dev[k]) for k in far_first(nz)],
            zr.at[t, pl.ds(1, nz - 1)],
        )

    def stage_end(t, hop):
        hop.wait_recv()
        share = zs[t, 0]
        for k in range(1, nz):
            share = share + zr[t, k]
        return share

    build_points(0)
    base0 = own_terms(0)
    rows0 = batch_rows(0)
    hop_xy = stage([(xy.at[0], xy.at[k], y_dev[k]) for k in far_first(ny)], xy.at[pl.ds(1, ny - 1)])
    prior0 = prior_part(rows0) + base0
    bulk.wait_recv()
    for k in range(1, ny):
        build_points(k)
    hop0 = partial(0, prior0)
    base1 = own_terms(1)
    rows1 = batch_rows(1)
    hop0 = stage_z(0, hop0)
    hop1 = partial(1, prior_part(rows1) + base1)
    vel0 = stage_end(0, hop0)
    vy[0] = vel0
    hop_vy = stage([(vy.at[0], vy.at[k], y_dev[k]) for k in far_first(ny)], vy.at[pl.ds(1, ny - 1)])
    vg[s] = vel0
    hop_g = stage([(vy.at[0], vg.at[s], s_dev[j]) for j in s_order], vg.at[pl.ds(1, ns - 1)])
    hop1 = stage_z(1, hop1)
    hop_xy.wait_recv()
    xa1 = xa[1]
    for k in range(ny):
        block = xy[k]
        pa0[k, 0:32, :] = block
        pa0[k, 32:48, :] = extra_rows(split_norm(block), TILE, 3)
        kc[k] = jnp.exp(dot00(pa0[k], xa1)).astype(BF16)
    hop_g.wait_recv()
    new0 = vg[...].reshape(64, TILE)
    mine, low = owned(0)
    for h in range(2):
        lanes = slice(h * TILE, (h + 1) * TILE)
        here = mine & (low == (h == 0))
        du[:, lanes] = jnp.where(here, new0, 0.0)
        dv[:, lanes] = jnp.where(here, new0 - vT[:, lanes], 0.0)
    share1 = stage_end(1, hop1)
    mine, low = owned(1)
    kept = momentum * (pick(vT, low) + pick(dv, low))

    hop_vy.wait_recv()
    corr = dot10(vy[0].astype(BF16), kc[0])
    for k in range(1, ny):
        corr = corr + dot10(vy[k].astype(BF16), kc[k])
    corr = corr * kv_scale
    cs[...] = corr[:, :TILE] + share1
    co[...] = corr[:, TILE:]
    fin[s] = cs[...]
    last = stage([(co, cr.at[s], p_dev[j]) for j in s_order + [0]], cr)
    last_s = stage([(cs, fin.at[s], s_dev[j]) for j in s_order], fin.at[pl.ds(1, ns - 1)])
    for whole in closing[:-2]:
        whole.wait_send()
    last.wait_recv()
    last_s.wait_recv()
    new1 = (fin[...] + cr[...]).reshape(64, TILE) + kept
    for h in range(2):
        lanes = slice(h * TILE, (h + 1) * TILE)
        here = mine & (low == (h == 0))
        du[:, lanes] = du[:, lanes] + jnp.where(here, new1, 0.0)
        dv[:, lanes] = jnp.where(here, new1 - vT[:, lanes], dv[:, lanes])
    last.wait_send()
    last_s.wait_send()


def local(
    nx, ny, nz,
    points, dual_weights, velocity, observed, noise_draws, frequencies, phases,
    prior_weights, batch_tiles,
):
    own, samples = dual_weights.shape
    feats = phases.shape[0]
    ns = nx * 2
    stages = 14
    vm = pltpu.VMEM
    share = samples // ns
    out = vm((samples, own), F32)
    add_u, add_v = pl.pallas_call(
        functools.partial(
            kernel, nx, ny, nz, own * nx * ny * nz * 2, feats * nx * nz
        ),
        out_shape=(out, out),
        in_specs=[pl.BlockSpec(memory_space=pl.ANY)] * 9,
        out_specs=(pl.BlockSpec(memory_space=pltpu.VMEM),) * 2,
        scratch_shapes=[
            pltpu.SMEM((STEPS,), jnp.int32),
            vm((samples, own), F32),
            vm((samples, own), F32),
            vm((1, own), F32),
            vm((samples, own), F32),
            vm((32, feats), BF16),
            vm((1, feats), F32),
            vm((samples, feats), BF16),
            vm((ny, 32 + samples, own), BF16),
            vm((ny, 48, own), BF16),
            vm((STEPS, 32, TILE), BF16),
            vm((STEPS, ns, 32, TILE), BF16),
            vm((STEPS, 32, TILE), BF16),
            vm((STEPS, nz, 32, TILE), BF16),
            vm((STEPS, 48, 2 * TILE), BF16),
            vm((ny, 32, TILE), BF16),
            vm((ny, 48, TILE), BF16),
            vm((ny, TILE, 2 * TILE), BF16),
            vm((STEPS, ns, share, 2 * TILE), F32),
            vm((STEPS, ns, share, 2 * TILE), F32),
            vm((STEPS, 2, share, TILE), F32),
            vm((STEPS, nz, share, TILE), F32),
            vm((ns, share, TILE), F32),
            vm((ny, share, TILE), F32),
            vm((share, TILE), F32),
            vm((share, TILE), F32),
            vm((ns, share, TILE), F32),
            vm((ns, share, TILE), F32),
            pltpu.SemaphoreType.DMA((9,)),
            pltpu.SemaphoreType.DMA((stages,)),
            pltpu.SemaphoreType.DMA((stages,)),
        ],
        compiler_params=pltpu.CompilerParams(collective_id=0, has_side_effects=True),
    )(
        batch_tiles.reshape(STEPS),
        points.T,
        dual_weights.T,
        velocity.T,
        observed.reshape(1, own),
        noise_draws.T,
        frequencies,
        phases.reshape(1, feats),
        prior_weights.T,
    )
    return dual_weights + add_u.T, velocity + add_v.T


def solution(mesh):
    nx = NX
    ny = mesh.shape["grp"] // 2
    nz = mesh.shape["feat"] // nx
    return jax.shard_map(
        functools.partial(local, nx, ny, nz),
        mesh=mesh,
        in_specs=(
            P(("grp", "feat"), None),
            P(("grp", "feat"), None),
            P(("grp", "feat"), None),
            P(("grp", "feat")),
            P(("grp", "feat"), None),
            P(None, "feat"),
            P("feat"),
            P("feat", None),
            P(None, "grp", None),
        ),
        out_specs=(P(("grp", "feat"), None), P(("grp", "feat"), None)),
        check_vma=False,
    )
```

```python
import functools
import math

import jax
import jax.numpy as jnp
from jax import lax
from jax.experimental import pallas as pl
from jax.experimental.pallas import tpu as pltpu
from jax.sharding import PartitionSpec as P

TILE = 128
STEPS = 2
NX = 4
MESH = pl.DeviceIdType.MESH

amplitude = 4.0
signal = 2.0
momentum = 0.9
step_size = 0.5

F32 = jnp.float32
BF16 = jnp.bfloat16

PI_HI = 3.140625
PI_LO = 9.67653589793e-4
INV_TWO_PI = 0.15915494309189535


def cosine(arg):
    turns = jnp.floor(arg * INV_TWO_PI + 0.5)
    half = arg * 0.5 - turns * PI_HI
    half = half - turns * PI_LO
    sq = half * half
    poly = sq * 2.6000493542416553e-06 + -0.00019806612414667135
    poly = poly * sq + 0.0083330172462401
    poly = poly * sq + -0.16666657094222279
    sine = half + half * (sq * poly)
    return 1.0 - 2.0 * (sine * sine)


def dot00(a, b):
    return lax.dot_general(a, b, (((0,), (0,)), ((), ())), preferred_element_type=F32)


def dot11(a, b):
    return lax.dot_general(a, b, (((1,), (1,)), ((), ())), preferred_element_type=F32)


def dot10(a, b):
    return lax.dot_general(a, b, (((1,), (0,)), ((), ())), preferred_element_type=F32)


def split_norm(cols):
    wide = cols.astype(F32)
    norm = jnp.sum(wide * wide, axis=0, keepdims=True) * (-1.0 / cols.shape[0])
    hi = norm.astype(BF16).astype(F32)
    rest = norm - hi
    mid = rest.astype(BF16).astype(F32)
    return hi, mid, rest - mid


def extra_rows(terms, width, first):
    rows = lax.broadcasted_iota(jnp.int32, (16, width), 0)
    out = jnp.where((rows >= 3 - first) & (rows < 6 - first), 1.0, 0.0)
    for i in range(3):
        out = jnp.where(rows == first + i, terms[i], out)
    return out.astype(BF16)


def kernel(
    nx, ny, nz, total_points, total_feats,
    bt_in, pT_in, uT_in, vT_in, ob_in, nT_in, fr_in, ph_in, wT_in,
    du, dv,
    bt, uT, vT, ob, nT, fr, ph, wT,
    gat, pa, xs1, xr1, xs2, xr2, xa, xy, pa0, kc, kk,
    pf, pr, zs, zr, zb, vg, vy, cs, co, fin, isem, ssem, rsem,
):
    nh = nz // 2
    ns = nx * 2
    loads = []
    for i, (src, dst) in enumerate((
        (bt_in, bt), (pT_in, gat.at[0, pl.ds(0, 32)]), (uT_in, uT), (fr_in, fr), (ph_in, ph),
        (wT_in, wT), (ob_in, ob), (nT_in, nT), (vT_in, vT),
    )):
        loads.append(pltpu.make_async_copy(src, dst, isem.at[i]))
        loads[-1].start()

    g = lax.axis_index("grp")
    f = lax.axis_index("feat")
    y = lax.div(g, 2)
    zl = lax.rem(g, 2)
    x = lax.div(f, nh * 2)
    c = lax.rem(f, 2)
    zh = lax.rem(lax.div(f, 2), nh)
    z = zh * 2 + zl
    s = x * 2 + c

    def at(s_, y_, z_):
        return {
            "grp": y_ * 2 + lax.rem(z_, 2),
            "feat": lax.div(s_, 2) * (nh * 2) + lax.div(z_, 2) * 2 + lax.rem(s_, 2),
        }

    def far_first(n):
        return sorted(range(1, n), key=lambda k: -min(k, n - k))

    block_of = {j: lax.rem(s + j, ns) for j in range(1, ns)}
    s_order = sorted(range(1, ns), key=lambda j: (-min(j, ns - j), j))
    s_dev = {j: at(block_of[j], y, z) for j in block_of}
    y_dev = {k: at(s, lax.rem(y + k, ny), z) for k in range(1, ny)}
    z_dev = {k: at(s, y, lax.rem(z + k, nz)) for k in range(1, nz)}

    barrier = pltpu.get_barrier_semaphore()
    greeted = [z_dev[k] for k in far_first(nz)] + [y_dev[k] for k in far_first(ny)]
    greeted += [s_dev[j] for j in s_order]
    for d in greeted:
        pl.semaphore_signal(barrier, inc=1, device_id=d, device_id_type=MESH)

    counts = [0, 0]
    closing = []

    def stage(copies, landing):
        i = counts[0]
        counts[0] += 1
        for src, dst, dev in copies:
            pltpu.make_async_remote_copy(
                src_ref=src, dst_ref=dst, send_sem=ssem.at[i], recv_sem=rsem.at[i],
                device_id=dev, device_id_type=MESH,
            ).start()
        whole = pltpu.make_async_remote_copy(
            src_ref=landing, dst_ref=landing, send_sem=ssem.at[i], recv_sem=rsem.at[i],
            device_id=copies[0][2], device_id_type=MESH,
        )
        closing.append(whole)
        return whole

    def owned(t):
        tile = bt[t]
        return lax.div(tile, 2) == f, lax.rem(tile, 2) == 0

    def pick(ref, low):
        return jnp.where(low, ref[:, :TILE], ref[:, TILE:])

    loads[0].wait()
    loads[1].wait()
    for t in range(STEPS):
        mine, low = owned(t)
        tile_rows = jnp.where(low, gat[0, 0:32, 0:TILE], gat[0, 0:32, TILE:])
        xs1[t] = jnp.where(mine, tile_rows.astype(F32), 0.0).astype(BF16)
    pl.semaphore_wait(barrier, len(greeted))

    hop_c = [
        stage([(xs1.at[t], xr1.at[t, j], s_dev[j]) for j in s_order], xr1.at[t, pl.ds(1, ns - 1)])
        for t in range(STEPS)
    ]
    rows_p, rows_d = pl.ds(0, 32), pl.ds(32, 64)
    others = pl.ds(1, ny - 1)
    bulk = stage(
        [(gat.at[0, rows_p], gat.at[k, rows_p], y_dev[k]) for k in far_first(ny)], gat.at[others, rows_p]
    )
    loads[2].wait()
    gat[0, 32:96, :] = uT[...].astype(BF16)
    bulk_d = stage(
        [(gat.at[0, rows_d], gat.at[k, rows_d], y_dev[k]) for k in far_first(ny)], gat.at[others, rows_d]
    )
    hop_d = []
    for t in range(STEPS):
        hop_c[t].wait_recv()
        acc = xs1[t]
        for j in range(1, ns):
            acc = acc + xr1[t, j]
        xs2[t] = acc
        hop_d.append(stage(
            [(xs2.at[t], xr2.at[t, k], z_dev[k]) for k in far_first(nz)], xr2.at[t, pl.ds(1, nz - 1)]
        ))
    for load in loads[3:]:
        load.wait()

    def build_points(k):
        block = gat[k, 0:32, :]
        pa[k, 0:32, :] = block
        pa[k, 32:48, :] = extra_rows(split_norm(block), 2 * TILE, 3)

    def batch_rows(t):
        hop_d[t].wait_recv()
        own = xs2[t]
        for k in range(2, nz, 2):
            own = own + xr2[t, k]
        oth = xr2[t, 1]
        for k in range(3, nz, 2):
            oth = oth + xr2[t, k]
        for i, rows in enumerate((own, oth)):
            lanes = slice(i * TILE, (i + 1) * TILE)
            if t == 0:
                xy[0, :, lanes] = rows
            xa[t, 0:32, lanes] = (rows.astype(F32) * (2.0 / 32)).astype(BF16)
            xa[t, 32:48, lanes] = extra_rows(split_norm(rows), TILE, 0)
        return own

    kv_scale = -step_size * amplitude / math.sqrt(total_points)
    prior_scale = -step_size * signal * math.sqrt(2.0 / total_feats)

    def prior_part(rows):
        feats = cosine(dot00(rows, fr[...]) + ph[...]).astype(BF16)
        return dot11(wT[...], feats) * prior_scale

    def kernel_part(t):
        xat = xa[t]
        if t == 0:
            for k in range(ny):
                kk[k] = jnp.exp(dot00(pa[k], xat)).astype(BF16)
            bulk_d.wait_recv()

        def one(k, acc):
            kern = kk[k] if t == 0 else jnp.exp(dot00(pa[k], xat)).astype(BF16)
            return acc + dot10(gat[k, 32:96, :], kern)

        return lax.fori_loop(0, ny, one, jnp.zeros((64, 2 * TILE), F32), unroll=True) * kv_scale

    def own_terms(t):
        mine, low = owned(t)
        terms = step_size * (pick(ob, low) - pick(nT, low))
        if t == 0:
            terms = terms + momentum * pick(vT, low)
        return jnp.where(mine, terms, 0.0)

    def partial(t, prior):
        part = kernel_part(t)
        own = part[:, :TILE] + prior
        pf[t, :, :, 0:TILE] = own.reshape(ns, 64 // ns, TILE)
        pf[t, :, :, TILE:] = part[:, TILE:].reshape(ns, 64 // ns, TILE)
        return stage(
            [(pf.at[t, block_of[j]], pr.at[t, j], s_dev[j]) for j in s_order],
            pr.at[t, pl.ds(1, ns - 1)],
        )

    def stage_z(t, hop):
        hop.wait_recv()
        share = pf[t, s]
        for j in range(1, ns):
            share = share + pr[t, j]
        if t == 0:
            zb[0] = share
            return stage(
                [(zb.at[0], zb.at[k], z_dev[k]) for k in far_first(nz)], zb.at[pl.ds(1, nz - 1)]
            )
        zs[0] = share[:, :TILE]
        zs[1] = share[:, TILE:]
        return stage(
            [(zs.at[k % 2], zr.at[k], z_dev[k]) for k in far_first(nz)], zr.at[pl.ds(1, nz - 1)]
        )

    def stage_end(t, hop):
        hop.wait_recv()
        if t == 0:
            even = sum((zb[k] for k in range(2, nz, 2)), zb[0])
            odd = sum((zb[k] for k in range(3, nz, 2)), zb[1])
            return even[:, :TILE] + odd[:, TILE:], even[:, TILE:] + odd[:, :TILE]
        return sum((zr[k] for k in range(1, nz)), zs[0])

    build_points(0)
    base0 = own_terms(0)
    bulk.wait_recv()
    for k in range(1, ny):
        build_points(k)
    rows0 = batch_rows(0)
    prior0 = prior_part(rows0) + base0
    hop0 = partial(0, prior0)
    hop_xy = stage([(xy.at[0], xy.at[k], y_dev[k]) for k in far_first(ny)], xy.at[pl.ds(1, ny - 1)])
    base1 = own_terms(1)
    rows1 = batch_rows(1)
    hop1 = partial(1, prior_part(rows1) + base1)
    hop0 = stage_z(0, hop0)
    hop1 = stage_z(1, hop1)
    hop_xy.wait_recv()
    xa1 = xa[1, :, 0:TILE]
    for k in range(ny):
        block = xy[k]
        pa0[k, 0:32, :] = block
        pa0[k, 32:48, :] = extra_rows(split_norm(block), 2 * TILE, 3)
        kc[k] = jnp.exp(dot00(pa0[k], xa1)).astype(BF16)
    vel0, vel0_oth = stage_end(0, hop0)
    vy[0, :, 0:TILE] = vel0.astype(BF16)
    vy[0, :, TILE:] = vel0_oth.astype(BF16)
    hop_vy = stage([(vy.at[0], vy.at[k], y_dev[k]) for k in far_first(ny)], vy.at[pl.ds(1, ny - 1)])
    co[...] = vel0
    vg[s] = vel0
    hop_g = stage([(co, vg.at[s], s_dev[j]) for j in s_order], vg.at[pl.ds(1, ns - 1)])
    hop_g.wait_recv()
    new0 = vg[...].reshape(64, TILE)
    mine, low = owned(0)
    for h in range(2):
        lanes = slice(h * TILE, (h + 1) * TILE)
        here = mine & (low == (h == 0))
        du[:, lanes] = jnp.where(here, new0, 0.0)
        dv[:, lanes] = jnp.where(here, new0 - vT[:, lanes], 0.0)
    share1 = stage_end(1, hop1)
    mine, low = owned(1)
    kept = momentum * (pick(vT, low) + pick(dv, low))

    hop_vy.wait_recv()
    corr = dot10(vy[0], kc[0])
    for k in range(1, ny):
        corr = corr + dot10(vy[k], kc[k])
    cs[...] = corr * kv_scale + share1
    fin[s] = cs[...]
    last = stage([(cs, fin.at[s], s_dev[j]) for j in s_order], fin.at[pl.ds(1, ns - 1)])
    for whole in closing[:-1]:
        whole.wait_send()
    last.wait_recv()
    new1 = fin[...].reshape(64, TILE) + kept
    for h in range(2):
        lanes = slice(h * TILE, (h + 1) * TILE)
        here = mine & (low == (h == 0))
        du[:, lanes] = du[:, lanes] + jnp.where(here, new1, 0.0)
        dv[:, lanes] = jnp.where(here, new1 - vT[:, lanes], dv[:, lanes])
    last.wait_send()


def local(
    nx, ny, nz,
    points, dual_weights, velocity, observed, noise_draws, frequencies, phases,
    prior_weights, batch_tiles,
):
    own, samples = dual_weights.shape
    feats = phases.shape[0]
    ns = nx * 2
    stages = 14
    vm = pltpu.VMEM
    share = samples // ns
    out = vm((samples, own), F32)
    add_u, add_v = pl.pallas_call(
        functools.partial(
            kernel, nx, ny, nz, own * nx * ny * nz * 2, feats * nx * nz
        ),
        out_shape=(out, out),
        in_specs=[pl.BlockSpec(memory_space=pl.ANY)] * 9,
        out_specs=(pl.BlockSpec(memory_space=pltpu.VMEM),) * 2,
        scratch_shapes=[
            pltpu.SMEM((STEPS,), jnp.int32),
            vm((samples, own), F32),
            vm((samples, own), F32),
            vm((1, own), F32),
            vm((samples, own), F32),
            vm((32, feats), BF16),
            vm((1, feats), F32),
            vm((samples, feats), BF16),
            vm((ny, 32 + samples, own), BF16),
            vm((ny, 48, own), BF16),
            vm((STEPS, 32, TILE), BF16),
            vm((STEPS, ns, 32, TILE), BF16),
            vm((STEPS, 32, TILE), BF16),
            vm((STEPS, nz, 32, TILE), BF16),
            vm((STEPS, 48, 2 * TILE), BF16),
            vm((ny, 32, 2 * TILE), BF16),
            vm((ny, 48, 2 * TILE), BF16),
            vm((ny, 2 * TILE, TILE), BF16),
            vm((ny, own, 2 * TILE), BF16),
            vm((STEPS, ns, share, 2 * TILE), F32),
            vm((STEPS, ns, share, 2 * TILE), F32),
            vm((2, share, TILE), F32),
            vm((nz, share, TILE), F32),
            vm((nz, share, 2 * TILE), F32),
            vm((ns, share, TILE), F32),
            vm((ny, share, 2 * TILE), BF16),
            vm((share, TILE), F32),
            vm((share, TILE), F32),
            vm((ns, share, TILE), F32),
            pltpu.SemaphoreType.DMA((9,)),
            pltpu.SemaphoreType.DMA((stages,)),
            pltpu.SemaphoreType.DMA((stages,)),
        ],
        compiler_params=pltpu.CompilerParams(collective_id=0, has_side_effects=True),
    )(
        batch_tiles.reshape(STEPS),
        points.T,
        dual_weights.T,
        velocity.T,
        observed.reshape(1, own),
        noise_draws.T,
        frequencies,
        phases.reshape(1, feats),
        prior_weights.T,
    )
    return dual_weights + add_u.T, velocity + add_v.T


def solution(mesh):
    nx = NX
    ny = mesh.shape["grp"] // 2
    nz = mesh.shape["feat"] // nx
    return jax.shard_map(
        functools.partial(local, nx, ny, nz),
        mesh=mesh,
        in_specs=(
            P(("grp", "feat"), None),
            P(("grp", "feat"), None),
            P(("grp", "feat"), None),
            P(("grp", "feat")),
            P(("grp", "feat"), None),
            P(None, "feat"),
            P("feat"),
            P("feat", None),
            P(None, "grp", None),
        ),
        out_specs=(P(("grp", "feat"), None), P(("grp", "feat"), None)),
        check_vma=False,
    )
```

```python
import functools
import math

import jax
import jax.numpy as jnp
from jax import lax
from jax.experimental import pallas as pl
from jax.experimental.pallas import tpu as pltpu
from jax.sharding import PartitionSpec as P

TILE = 128
STEPS = 2
NX = 4
MESH = pl.DeviceIdType.MESH

amplitude = 4.0
signal = 2.0
momentum = 0.9
step_size = 0.5

F32 = jnp.float32
BF16 = jnp.bfloat16

PI_HI = 3.140625
PI_LO = 9.67653589793e-4
INV_TWO_PI = 0.15915494309189535


def cosine(arg):
    turns = jnp.floor(arg * INV_TWO_PI + 0.5)
    half = arg * 0.5 - turns * PI_HI
    half = half - turns * PI_LO
    sq = half * half
    poly = sq * 2.6000493542416553e-06 + -0.00019806612414667135
    poly = poly * sq + 0.0083330172462401
    poly = poly * sq + -0.16666657094222279
    sine = half + half * (sq * poly)
    return 1.0 - 2.0 * (sine * sine)


def dot00(a, b):
    return lax.dot_general(a, b, (((0,), (0,)), ((), ())), preferred_element_type=F32)


def dot11(a, b):
    return lax.dot_general(a, b, (((1,), (1,)), ((), ())), preferred_element_type=F32)


def dot10(a, b):
    return lax.dot_general(a, b, (((1,), (0,)), ((), ())), preferred_element_type=F32)


def split_norm(cols):
    wide = cols.astype(F32)
    norm = jnp.sum(wide * wide, axis=0, keepdims=True) * (-1.0 / cols.shape[0])
    hi = norm.astype(BF16).astype(F32)
    rest = norm - hi
    mid = rest.astype(BF16).astype(F32)
    return hi, mid, rest - mid


def extra_rows(terms, width, first):
    rows = lax.broadcasted_iota(jnp.int32, (16, width), 0)
    out = jnp.where((rows >= 3 - first) & (rows < 6 - first), 1.0, 0.0)
    for i in range(3):
        out = jnp.where(rows == first + i, terms[i], out)
    return out.astype(BF16)


def kernel(
    nx, ny, nz, total_points, total_feats,
    bt_in, pT_in, uT_in, vT_in, ob_in, nT_in, fr_in, ph_in, wT_in,
    du, dv,
    bt, uT, vT, ob, nT, fr, ph, wT,
    gat, pa, xs1, xr1, xs2, xr2, xa, xy, pa0, kc, kk,
    pf, pr, zs, zr, vg, vy, cs, sg, fz, isem, ssem, rsem,
):
    nh = nz // 2
    ns = nx * 2
    loads = []
    for i, (src, dst) in enumerate((
        (bt_in, bt), (pT_in, gat.at[0, pl.ds(0, 32)]), (uT_in, uT), (fr_in, fr), (ph_in, ph),
        (wT_in, wT), (ob_in, ob), (nT_in, nT), (vT_in, vT),
    )):
        loads.append(pltpu.make_async_copy(src, dst, isem.at[i]))
        loads[-1].start()

    g = lax.axis_index("grp")
    f = lax.axis_index("feat")
    y = lax.div(g, 2)
    zl = lax.rem(g, 2)
    x = lax.div(f, nh * 2)
    c = lax.rem(f, 2)
    zh = lax.rem(lax.div(f, 2), nh)
    z = zh * 2 + zl
    s = x * 2 + c

    def at(s_, y_, z_):
        return {
            "grp": y_ * 2 + lax.rem(z_, 2),
            "feat": lax.div(s_, 2) * (nh * 2) + lax.div(z_, 2) * 2 + lax.rem(s_, 2),
        }

    def far_first(n):
        return sorted(range(1, n), key=lambda k: -min(k, n - k))

    block_of = {j: lax.rem(s + j, ns) for j in range(1, ns)}
    s_order = sorted(range(1, ns), key=lambda j: (-min(j, ns - j), j))
    s_dev = {j: at(block_of[j], y, z) for j in block_of}
    y_dev = {k: at(s, lax.rem(y + k, ny), z) for k in range(1, ny)}
    z_dev = {k: at(s, y, lax.rem(z + k, nz)) for k in range(1, nz)}

    barrier = pltpu.get_barrier_semaphore()
    greeted = [z_dev[k] for k in far_first(nz)] + [y_dev[k] for k in far_first(ny)]
    greeted += [s_dev[j] for j in s_order]
    for d in greeted:
        pl.semaphore_signal(barrier, inc=1, device_id=d, device_id_type=MESH)

    counts = [0, 0]
    closing = []

    def stage(copies, landing):
        i = counts[0]
        counts[0] += 1
        for src, dst, dev in copies:
            pltpu.make_async_remote_copy(
                src_ref=src, dst_ref=dst, send_sem=ssem.at[i], recv_sem=rsem.at[i],
                device_id=dev, device_id_type=MESH,
            ).start()
        whole = pltpu.make_async_remote_copy(
            src_ref=landing, dst_ref=landing, send_sem=ssem.at[i], recv_sem=rsem.at[i],
            device_id=copies[0][2], device_id_type=MESH,
        )
        closing.append(whole)
        return whole

    def owned(t):
        tile = bt[t]
        return lax.div(tile, 2) == f, lax.rem(tile, 2) == 0

    def pick(ref, low):
        return jnp.where(low, ref[:, :TILE], ref[:, TILE:])

    loads[0].wait()
    loads[1].wait()
    for t in range(STEPS):
        mine, low = owned(t)
        tile_rows = jnp.where(low, gat[0, 0:32, 0:TILE], gat[0, 0:32, TILE:])
        xs1[t] = jnp.where(mine, tile_rows.astype(F32), 0.0).astype(BF16)
    pl.semaphore_wait(barrier, len(greeted))

    hop_c = [
        stage([(xs1.at[t], xr1.at[t, j], s_dev[j]) for j in s_order], xr1.at[t, pl.ds(1, ns - 1)])
        for t in range(STEPS)
    ]
    rows_p, rows_d = pl.ds(0, 32), pl.ds(32, 64)
    others = pl.ds(1, ny - 1)
    bulk = stage(
        [(gat.at[0, rows_p], gat.at[k, rows_p], y_dev[k]) for k in far_first(ny)], gat.at[others, rows_p]
    )
    loads[2].wait()
    gat[0, 32:96, :] = uT[...].astype(BF16)
    bulk_d = stage(
        [(gat.at[0, rows_d], gat.at[k, rows_d], y_dev[k]) for k in far_first(ny)], gat.at[others, rows_d]
    )
    hop_d = []
    for t in range(STEPS):
        hop_c[t].wait_recv()
        acc = xs1[t]
        for j in range(1, ns):
            acc = acc + xr1[t, j]
        xs2[t] = acc
        hop_d.append(stage(
            [(xs2.at[t], xr2.at[t, k], z_dev[k]) for k in far_first(nz)], xr2.at[t, pl.ds(1, nz - 1)]
        ))
    for load in loads[3:]:
        load.wait()

    def build_points(k):
        block = gat[k, 0:32, :]
        pa[k, 0:32, :] = block
        pa[k, 32:48, :] = extra_rows(split_norm(block), 2 * TILE, 3)

    def batch_rows(t):
        hop_d[t].wait_recv()
        own = xs2[t]
        for k in range(2, nz, 2):
            own = own + xr2[t, k]
        oth = xr2[t, 1]
        for k in range(3, nz, 2):
            oth = oth + xr2[t, k]
        for i, rows in enumerate((own, oth)):
            lanes = slice(i * TILE, (i + 1) * TILE)
            if t == 0:
                xy[0, :, lanes] = rows
            xa[t, 0:32, lanes] = (rows.astype(F32) * (2.0 / 32)).astype(BF16)
            xa[t, 32:48, lanes] = extra_rows(split_norm(rows), TILE, 0)
        return own

    kv_scale = -step_size * amplitude / math.sqrt(total_points)
    prior_scale = -step_size * signal * math.sqrt(2.0 / total_feats)

    def prior_part(rows):
        feats = cosine(dot00(rows, fr[...]) + ph[...]).astype(BF16)
        return dot11(wT[...], feats) * prior_scale

    def kernel_part(t):
        xat = xa[t]
        if t == 0:
            for k in range(ny):
                kk[k] = jnp.exp(dot00(pa[k], xat)).astype(BF16)
            bulk_d.wait_recv()

        def one(k, acc):
            kern = kk[k] if t == 0 else jnp.exp(dot00(pa[k], xat)).astype(BF16)
            return acc + dot10(gat[k, 32:96, :], kern)

        return lax.fori_loop(0, ny, one, jnp.zeros((64, 2 * TILE), F32), unroll=True) * kv_scale

    def own_terms(t):
        mine, low = owned(t)
        terms = step_size * (pick(ob, low) - pick(nT, low))
        if t == 0:
            terms = terms + momentum * pick(vT, low)
        return jnp.where(mine, terms, 0.0)

    def partial(t, prior):
        part = kernel_part(t)
        own = part[:, :TILE] + prior
        pf[t, :, :, 0:TILE] = own.reshape(ns, 64 // ns, TILE)
        pf[t, :, :, TILE:] = part[:, TILE:].reshape(ns, 64 // ns, TILE)
        return stage(
            [(pf.at[t, block_of[j]], pr.at[t, j], s_dev[j]) for j in s_order],
            pr.at[t, pl.ds(1, ns - 1)],
        )

    def stage_z(t, hop):
        hop.wait_recv()
        share = pf[t, s]
        for j in range(1, ns):
            share = share + pr[t, j]
        hop = None
        if t == 0:
            vy[0] = share.astype(BF16)
            hop = stage([(vy.at[0], vy.at[k], y_dev[k]) for k in far_first(ny)], vy.at[pl.ds(1, ny - 1)])
        zs[t, 0] = share[:, :TILE]
        zs[t, 1] = share[:, TILE:]
        return hop, stage(
            [(zs.at[t, k % 2], zr.at[t, k], z_dev[k]) for k in far_first(nz)],
            zr.at[t, pl.ds(1, nz - 1)],
        )

    def stage_end(t, hop):
        hop.wait_recv()
        return sum((zr[t, k] for k in range(1, nz)), zs[t, 0])

    def gather_shares(t, share):
        sg[t] = share
        vg[t, s] = share
        return stage(
            [(sg.at[t], vg.at[t, s], s_dev[j]) for j in s_order], vg.at[t, pl.ds(1, ns - 1)]
        )

    build_points(0)
    base0 = own_terms(0)
    bulk.wait_recv()
    for k in range(1, ny):
        build_points(k)
    rows0 = batch_rows(0)
    prior0 = prior_part(rows0) + base0
    hop0 = partial(0, prior0)
    hop_xy = stage([(xy.at[0], xy.at[k], y_dev[k]) for k in far_first(ny)], xy.at[pl.ds(1, ny - 1)])
    base1 = own_terms(1)
    rows1 = batch_rows(1)
    hop1 = partial(1, prior_part(rows1) + base1)
    hop_vy, hop0 = stage_z(0, hop0)
    hop1 = stage_z(1, hop1)[1]
    hop_xy.wait_recv()
    xa1 = xa[1]
    for k in range(ny):
        block = xy[k]
        pa0[k, 0:32, :] = block
        pa0[k, 32:48, :] = extra_rows(split_norm(block), 2 * TILE, 3)
        kc[k] = jnp.exp(dot00(pa0[k], xa1)).astype(BF16)

    hop_vy.wait_recv()
    corr = dot10(vy[0], kc[0])
    for k in range(1, ny):
        corr = corr + dot10(vy[k], kc[k])
    corr = (corr * kv_scale).astype(BF16)
    cs[0] = corr[:, :TILE]
    cs[1] = corr[:, TILE:]
    fz[0, s] = corr[:, :TILE]
    copies = [
        (cs.at[k % 2], fz.at[k, s], at(s if j == 0 else block_of[j], y, lax.rem(z + k, nz)))
        for k in far_first(nz) for j in s_order + [0]
    ]
    last = stage(copies, fz.at[pl.ds(1, nz - 1)])
    last_s = stage([(cs.at[0], fz.at[0, s], s_dev[j]) for j in s_order], fz.at[0, pl.ds(1, ns - 1)])

    hop_g0 = gather_shares(0, stage_end(0, hop0))
    hop_g1 = gather_shares(1, stage_end(1, hop1))
    hop_g0.wait_recv()
    new0 = vg[0].reshape(64, TILE)
    mine, low = owned(0)
    for h in range(2):
        lanes = slice(h * TILE, (h + 1) * TILE)
        here = mine & (low == (h == 0))
        du[:, lanes] = jnp.where(here, new0, 0.0)
        dv[:, lanes] = jnp.where(here, new0 - vT[:, lanes], 0.0)
    mine, low = owned(1)
    kept = momentum * (pick(vT, low) + pick(dv, low))
    hop_g1.wait_recv()
    kept = kept + vg[1].reshape(64, TILE)
    for whole in closing:
        whole.wait_send()
    last.wait_recv()
    last_s.wait_recv()
    new1 = sum((fz[k].astype(F32) for k in range(1, nz)), fz[0].astype(F32)).reshape(64, TILE) + kept
    for h in range(2):
        lanes = slice(h * TILE, (h + 1) * TILE)
        here = mine & (low == (h == 0))
        du[:, lanes] = du[:, lanes] + jnp.where(here, new1, 0.0)
        dv[:, lanes] = jnp.where(here, new1 - vT[:, lanes], dv[:, lanes])


def local(
    nx, ny, nz,
    points, dual_weights, velocity, observed, noise_draws, frequencies, phases,
    prior_weights, batch_tiles,
):
    own, samples = dual_weights.shape
    feats = phases.shape[0]
    ns = nx * 2
    stages = 16
    vm = pltpu.VMEM
    share = samples // ns
    out = vm((samples, own), F32)
    add_u, add_v = pl.pallas_call(
        functools.partial(
            kernel, nx, ny, nz, own * nx * ny * nz * 2, feats * nx * nz
        ),
        out_shape=(out, out),
        in_specs=[pl.BlockSpec(memory_space=pl.ANY)] * 9,
        out_specs=(pl.BlockSpec(memory_space=pltpu.VMEM),) * 2,
        scratch_shapes=[
            pltpu.SMEM((STEPS,), jnp.int32),
            vm((samples, own), F32),
            vm((samples, own), F32),
            vm((1, own), F32),
            vm((samples, own), F32),
            vm((32, feats), BF16),
            vm((1, feats), F32),
            vm((samples, feats), BF16),
            vm((ny, 32 + samples, own), BF16),
            vm((ny, 48, own), BF16),
            vm((STEPS, 32, TILE), BF16),
            vm((STEPS, ns, 32, TILE), BF16),
            vm((STEPS, 32, TILE), BF16),
            vm((STEPS, nz, 32, TILE), BF16),
            vm((STEPS, 48, 2 * TILE), BF16),
            vm((ny, 32, 2 * TILE), BF16),
            vm((ny, 48, 2 * TILE), BF16),
            vm((ny, 2 * TILE, 2 * TILE), BF16),
            vm((ny, own, 2 * TILE), BF16),
            vm((STEPS, ns, share, 2 * TILE), F32),
            vm((STEPS, ns, share, 2 * TILE), F32),
            vm((STEPS, 2, share, TILE), F32),
            vm((STEPS, nz, share, TILE), F32),
            vm((STEPS, ns, share, TILE), F32),
            vm((ny, share, 2 * TILE), BF16),
            vm((2, share, TILE), BF16),
            vm((STEPS, share, TILE), F32),
            vm((nz, ns, share, TILE), BF16),
            pltpu.SemaphoreType.DMA((9,)),
            pltpu.SemaphoreType.DMA((stages,)),
            pltpu.SemaphoreType.DMA((stages,)),
        ],
        compiler_params=pltpu.CompilerParams(collective_id=0, has_side_effects=True),
    )(
        batch_tiles.reshape(STEPS),
        points.T,
        dual_weights.T,
        velocity.T,
        observed.reshape(1, own),
        noise_draws.T,
        frequencies,
        phases.reshape(1, feats),
        prior_weights.T,
    )
    return dual_weights + add_u.T, velocity + add_v.T


def solution(mesh):
    nx = NX
    ny = mesh.shape["grp"] // 2
    nz = mesh.shape["feat"] // nx
    return jax.shard_map(
        functools.partial(local, nx, ny, nz),
        mesh=mesh,
        in_specs=(
            P(("grp", "feat"), None),
            P(("grp", "feat"), None),
            P(("grp", "feat"), None),
            P(("grp", "feat")),
            P(("grp", "feat"), None),
            P(None, "feat"),
            P("feat"),
            P("feat", None),
            P(None, "grp", None),
        ),
        out_specs=(P(("grp", "feat"), None), P(("grp", "feat"), None)),
        check_vma=False,
    )
```

```python
import functools
import math

import jax
import jax.numpy as jnp
from jax import lax
from jax.experimental import pallas as pl
from jax.experimental.pallas import tpu as pltpu
from jax.sharding import PartitionSpec as P

TILE = 128
STEPS = 2
NX = 4
MESH = pl.DeviceIdType.MESH

amplitude = 4.0
signal = 2.0
momentum = 0.9
step_size = 0.5

F32 = jnp.float32
BF16 = jnp.bfloat16

PI_HI = 3.140625
PI_LO = 9.67653589793e-4
INV_TWO_PI = 0.15915494309189535


def cosine(arg):
    turns = jnp.floor(arg * INV_TWO_PI + 0.5)
    half = arg * 0.5 - turns * PI_HI
    half = half - turns * PI_LO
    sq = half * half
    poly = sq * 2.6000493542416553e-06 + -0.00019806612414667135
    poly = poly * sq + 0.0083330172462401
    poly = poly * sq + -0.16666657094222279
    sine = half + half * (sq * poly)
    return 1.0 - 2.0 * (sine * sine)


def dot00(a, b):
    return lax.dot_general(a, b, (((0,), (0,)), ((), ())), preferred_element_type=F32)


def dot11(a, b):
    return lax.dot_general(a, b, (((1,), (1,)), ((), ())), preferred_element_type=F32)


def dot10(a, b):
    return lax.dot_general(a, b, (((1,), (0,)), ((), ())), preferred_element_type=F32)


def split_norm(cols):
    wide = cols.astype(F32)
    norm = jnp.sum(wide * wide, axis=0, keepdims=True) * (-1.0 / cols.shape[0])
    hi = norm.astype(BF16).astype(F32)
    rest = norm - hi
    mid = rest.astype(BF16).astype(F32)
    return hi, mid, rest - mid


def extra_rows(terms, width, first):
    rows = lax.broadcasted_iota(jnp.int32, (16, width), 0)
    out = jnp.where((rows >= 3 - first) & (rows < 6 - first), 1.0, 0.0)
    for i in range(3):
        out = jnp.where(rows == first + i, terms[i], out)
    return out.astype(BF16)


def kernel(
    nx, ny, nz, total_points, total_feats,
    bt_in, pT_in, uT_in, vT_in, ob_in, nT_in, fr_in, ph_in, wT_in,
    du, dv,
    bt, uT, vT, ob, nT, fr, ph, wT,
    gat, pa, xs1, xr1, xs2, xr2, xa, xy, pa0, kc, kk,
    pf, pr, zs, zr, vg, vy, cs, sg, fz, isem, ssem, rsem,
):
    nh = nz // 2
    ns = nx * 2
    loads = []
    for i, (src, dst) in enumerate((
        (bt_in, bt), (pT_in, gat.at[0, pl.ds(0, 32)]), (uT_in, uT), (fr_in, fr), (ph_in, ph),
        (wT_in, wT), (ob_in, ob), (nT_in, nT), (vT_in, vT),
    )):
        loads.append(pltpu.make_async_copy(src, dst, isem.at[i]))
        loads[-1].start()

    g = lax.axis_index("grp")
    f = lax.axis_index("feat")
    y = lax.div(g, 2)
    zl = lax.rem(g, 2)
    x = lax.div(f, nh * 2)
    c = lax.rem(f, 2)
    zh = lax.rem(lax.div(f, 2), nh)
    z = zh * 2 + zl
    s = x * 2 + c

    def at(s_, y_, z_):
        return {
            "grp": y_ * 2 + lax.rem(z_, 2),
            "feat": lax.div(s_, 2) * (nh * 2) + lax.div(z_, 2) * 2 + lax.rem(s_, 2),
        }

    def far_first(n):
        return sorted(range(1, n), key=lambda k: -min(k, n - k))

    block_of = {j: lax.rem(s + j, ns) for j in range(1, ns)}
    s_order = sorted(range(1, ns), key=lambda j: (-min(j, ns - j), j))
    s_dev = {j: at(block_of[j], y, z) for j in block_of}
    y_dev = {k: at(s, lax.rem(y + k, ny), z) for k in range(1, ny)}
    z_dev = {k: at(s, y, lax.rem(z + k, nz)) for k in range(1, nz)}

    barrier = pltpu.get_barrier_semaphore()
    greeted = [z_dev[k] for k in far_first(nz)] + [y_dev[k] for k in far_first(ny)]
    greeted += [s_dev[j] for j in s_order]
    for d in greeted:
        pl.semaphore_signal(barrier, inc=1, device_id=d, device_id_type=MESH)

    counts = [0, 0]
    closing = []

    def stage(copies, landing):
        i = counts[0]
        counts[0] += 1
        for src, dst, dev in copies:
            pltpu.make_async_remote_copy(
                src_ref=src, dst_ref=dst, send_sem=ssem.at[i], recv_sem=rsem.at[i],
                device_id=dev, device_id_type=MESH,
            ).start()
        whole = pltpu.make_async_remote_copy(
            src_ref=landing, dst_ref=landing, send_sem=ssem.at[i], recv_sem=rsem.at[i],
            device_id=copies[0][2], device_id_type=MESH,
        )
        closing.append(whole)
        return whole

    def owned(t):
        tile = bt[t]
        return lax.div(tile, 2) == f, lax.rem(tile, 2) == 0

    def pick(ref, low):
        return jnp.where(low, ref[:, :TILE], ref[:, TILE:])

    loads[0].wait()
    loads[1].wait()
    for t in range(STEPS):
        mine, low = owned(t)
        tile_rows = jnp.where(low, gat[0, 0:32, 0:TILE], gat[0, 0:32, TILE:])
        xs1[t] = jnp.where(mine, tile_rows.astype(F32), 0.0).astype(BF16)
    pl.semaphore_wait(barrier, len(greeted))

    hop_c = [
        stage([(xs1.at[t], xr1.at[t, j], s_dev[j]) for j in s_order], xr1.at[t, pl.ds(1, ns - 1)])
        for t in range(STEPS)
    ]
    rows_p, rows_d = pl.ds(0, 32), pl.ds(32, 64)
    others = pl.ds(1, ny - 1)
    bulk = stage(
        [(gat.at[0, rows_p], gat.at[k, rows_p], y_dev[k]) for k in far_first(ny)], gat.at[others, rows_p]
    )
    loads[2].wait()
    gat[0, 32:96, :] = uT[...].astype(BF16)
    bulk_d = stage(
        [(gat.at[0, rows_d], gat.at[k, rows_d], y_dev[k]) for k in far_first(ny)], gat.at[others, rows_d]
    )
    hop_d = []
    for t in range(STEPS):
        hop_c[t].wait_recv()
        acc = xs1[t]
        for j in range(1, ns):
            acc = acc + xr1[t, j]
        xs2[t] = acc
        hop_d.append(stage(
            [(xs2.at[t], xr2.at[t, k], z_dev[k]) for k in far_first(nz)], xr2.at[t, pl.ds(1, nz - 1)]
        ))
    for load in loads[3:]:
        load.wait()

    def build_points(k):
        block = gat[k, 0:32, :]
        pa[k, 0:32, :] = block
        pa[k, 32:48, :] = extra_rows(split_norm(block), 2 * TILE, 3)

    def batch_rows(t):
        hop_d[t].wait_recv()
        own = xs2[t]
        for k in range(2, nz, 2):
            own = own + xr2[t, k]
        oth = xr2[t, 1]
        for k in range(3, nz, 2):
            oth = oth + xr2[t, k]
        for i, rows in enumerate((own, oth)):
            lanes = slice(i * TILE, (i + 1) * TILE)
            if t == 0:
                xy[0, :, lanes] = rows
            xa[t, 0:32, lanes] = (rows.astype(F32) * (2.0 / 32)).astype(BF16)
            xa[t, 32:48, lanes] = extra_rows(split_norm(rows), TILE, 0)
        return own

    kv_scale = -step_size * amplitude / math.sqrt(total_points)
    prior_scale = -step_size * signal * math.sqrt(2.0 / total_feats)

    def prior_part(rows):
        feats = cosine(dot00(rows, fr[...]) + ph[...]).astype(BF16)
        return dot11(wT[...], feats) * prior_scale

    def kernel_part(t):
        xat = xa[t]
        if t == 0:
            for k in range(ny // 2):
                kk[k] = jnp.exp(dot00(pa[k], xat)).astype(BF16)
            bulk_d.wait_recv()
            acc = jnp.zeros((64, 2 * TILE), F32)
            for k in range(ny):
                kern = kk[k] if k < ny // 2 else jnp.exp(dot00(pa[k], xat)).astype(BF16)
                acc = acc + dot10(gat[k, 32:96, :], kern)
            return acc * kv_scale

        def one(k, acc):
            kern = jnp.exp(dot00(pa[k], xat)).astype(BF16)
            return acc + dot10(gat[k, 32:96, :], kern)

        return lax.fori_loop(0, ny, one, jnp.zeros((64, 2 * TILE), F32), unroll=True) * kv_scale

    def own_terms(t):
        mine, low = owned(t)
        terms = step_size * (pick(ob, low) - pick(nT, low))
        if t == 0:
            terms = terms + momentum * pick(vT, low)
        return jnp.where(mine, terms, 0.0)

    def partial(t, prior):
        part = kernel_part(t)
        own = part[:, :TILE] + prior
        pf[t, :, :, 0:TILE] = own.reshape(ns, 64 // ns, TILE)
        pf[t, :, :, TILE:] = part[:, TILE:].reshape(ns, 64 // ns, TILE)
        return stage(
            [(pf.at[t, block_of[j]], pr.at[t, j], s_dev[j]) for j in s_order],
            pr.at[t, pl.ds(1, ns - 1)],
        )

    def stage_z(t, hop):
        hop.wait_recv()
        share = pf[t, s]
        for j in range(1, ns):
            share = share + pr[t, j]
        hop = None
        if t == 0:
            vy[0] = share.astype(BF16)
            hop = stage([(vy.at[0], vy.at[k], y_dev[k]) for k in far_first(ny)], vy.at[pl.ds(1, ny - 1)])
        zs[t, 0] = share[:, :TILE]
        zs[t, 1] = share[:, TILE:]
        return hop, stage(
            [(zs.at[t, k % 2], zr.at[t, k], z_dev[k]) for k in far_first(nz)],
            zr.at[t, pl.ds(1, nz - 1)],
        )

    def stage_end(t, hop):
        hop.wait_recv()
        return sum((zr[t, k] for k in range(1, nz)), zs[t, 0])

    def gather_shares(t, share):
        sg[t] = share
        vg[t, s] = share
        return stage(
            [(sg.at[t], vg.at[t, s], s_dev[j]) for j in s_order], vg.at[t, pl.ds(1, ns - 1)]
        )

    build_points(0)
    base0 = own_terms(0)
    bulk.wait_recv()
    for k in range(1, ny):
        build_points(k)
    rows0 = batch_rows(0)
    prior0 = prior_part(rows0) + base0
    hop0 = partial(0, prior0)
    hop_xy = stage([(xy.at[0], xy.at[k], y_dev[k]) for k in far_first(ny)], xy.at[pl.ds(1, ny - 1)])
    base1 = own_terms(1)
    rows1 = batch_rows(1)
    hop1 = partial(1, prior_part(rows1) + base1)
    hop_vy, hop0 = stage_z(0, hop0)
    hop1 = stage_z(1, hop1)[1]
    hop_xy.wait_recv()
    xa1 = xa[1]
    for k in range(ny):
        block = xy[k]
        pa0[k, 0:32, :] = block
        pa0[k, 32:48, :] = extra_rows(split_norm(block), 2 * TILE, 3)
        kc[k] = jnp.exp(dot00(pa0[k], xa1)).astype(BF16)

    hop_vy.wait_recv()
    corr = dot10(vy[0], kc[0])
    for k in range(1, ny):
        corr = corr + dot10(vy[k], kc[k])
    corr = (corr * kv_scale).astype(BF16)
    cs[0] = corr[:, :TILE]
    cs[1] = corr[:, TILE:]
    fz[0, s] = corr[:, :TILE]
    copies = [
        (cs.at[k % 2], fz.at[k, s], at(s if j == 0 else block_of[j], y, lax.rem(z + k, nz)))
        for j in s_order + [0] for k in far_first(nz)
    ]
    last = stage(copies, fz.at[pl.ds(1, nz - 1)])
    last_s = stage([(cs.at[0], fz.at[0, s], s_dev[j]) for j in s_order], fz.at[0, pl.ds(1, ns - 1)])

    hop_g0 = gather_shares(0, stage_end(0, hop0))
    hop_g1 = gather_shares(1, stage_end(1, hop1))
    hop_g0.wait_recv()
    new0 = vg[0].reshape(64, TILE)
    mine, low = owned(0)
    for h in range(2):
        lanes = slice(h * TILE, (h + 1) * TILE)
        here = mine & (low == (h == 0))
        du[:, lanes] = jnp.where(here, new0, 0.0)
        dv[:, lanes] = jnp.where(here, new0 - vT[:, lanes], 0.0)
    mine, low = owned(1)
    kept = momentum * (pick(vT, low) + pick(dv, low))
    hop_g1.wait_recv()
    kept = kept + vg[1].reshape(64, TILE)
    for whole in closing:
        whole.wait_send()
    last.wait_recv()
    last_s.wait_recv()
    new1 = sum((fz[k].astype(F32) for k in range(1, nz)), fz[0].astype(F32)).reshape(64, TILE) + kept
    for h in range(2):
        lanes = slice(h * TILE, (h + 1) * TILE)
        here = mine & (low == (h == 0))
        du[:, lanes] = du[:, lanes] + jnp.where(here, new1, 0.0)
        dv[:, lanes] = jnp.where(here, new1 - vT[:, lanes], dv[:, lanes])


def local(
    nx, ny, nz,
    points, dual_weights, velocity, observed, noise_draws, frequencies, phases,
    prior_weights, batch_tiles,
):
    own, samples = dual_weights.shape
    feats = phases.shape[0]
    ns = nx * 2
    stages = 16
    vm = pltpu.VMEM
    share = samples // ns
    out = vm((samples, own), F32)
    add_u, add_v = pl.pallas_call(
        functools.partial(
            kernel, nx, ny, nz, own * nx * ny * nz * 2, feats * nx * nz
        ),
        out_shape=(out, out),
        in_specs=[pl.BlockSpec(memory_space=pl.ANY)] * 9,
        out_specs=(pl.BlockSpec(memory_space=pltpu.VMEM),) * 2,
        scratch_shapes=[
            pltpu.SMEM((STEPS,), jnp.int32),
            vm((samples, own), F32),
            vm((samples, own), F32),
            vm((1, own), F32),
            vm((samples, own), F32),
            vm((32, feats), BF16),
            vm((1, feats), F32),
            vm((samples, feats), BF16),
            vm((ny, 32 + samples, own), BF16),
            vm((ny, 48, own), BF16),
            vm((STEPS, 32, TILE), BF16),
            vm((STEPS, ns, 32, TILE), BF16),
            vm((STEPS, 32, TILE), BF16),
            vm((STEPS, nz, 32, TILE), BF16),
            vm((STEPS, 48, 2 * TILE), BF16),
            vm((ny, 32, 2 * TILE), BF16),
            vm((ny, 48, 2 * TILE), BF16),
            vm((ny, 2 * TILE, 2 * TILE), BF16),
            vm((ny, own, 2 * TILE), BF16),
            vm((STEPS, ns, share, 2 * TILE), F32),
            vm((STEPS, ns, share, 2 * TILE), F32),
            vm((STEPS, 2, share, TILE), F32),
            vm((STEPS, nz, share, TILE), F32),
            vm((STEPS, ns, share, TILE), F32),
            vm((ny, share, 2 * TILE), BF16),
            vm((2, share, TILE), BF16),
            vm((STEPS, share, TILE), F32),
            vm((nz, ns, share, TILE), BF16),
            pltpu.SemaphoreType.DMA((9,)),
            pltpu.SemaphoreType.DMA((stages,)),
            pltpu.SemaphoreType.DMA((stages,)),
        ],
        compiler_params=pltpu.CompilerParams(collective_id=0, has_side_effects=True),
    )(
        batch_tiles.reshape(STEPS),
        points.T,
        dual_weights.T,
        velocity.T,
        observed.reshape(1, own),
        noise_draws.T,
        frequencies,
        phases.reshape(1, feats),
        prior_weights.T,
    )
    return dual_weights + add_u.T, velocity + add_v.T


def solution(mesh):
    nx = NX
    ny = mesh.shape["grp"] // 2
    nz = mesh.shape["feat"] // nx
    return jax.shard_map(
        functools.partial(local, nx, ny, nz),
        mesh=mesh,
        in_specs=(
            P(("grp", "feat"), None),
            P(("grp", "feat"), None),
            P(("grp", "feat"), None),
            P(("grp", "feat")),
            P(("grp", "feat"), None),
            P(None, "feat"),
            P("feat"),
            P("feat", None),
            P(None, "grp", None),
        ),
        out_specs=(P(("grp", "feat"), None), P(("grp", "feat"), None)),
        check_vma=False,
    )
```

```python
import functools
import math

import jax
import jax.numpy as jnp
from jax import lax
from jax.experimental import pallas as pl
from jax.experimental.pallas import tpu as pltpu
from jax.sharding import PartitionSpec as P

TILE = 128
STEPS = 2
NX = 4
MESH = pl.DeviceIdType.MESH

amplitude = 4.0
signal = 2.0
momentum = 0.9
step_size = 0.5

F32 = jnp.float32
BF16 = jnp.bfloat16

PI_HI = 3.140625
PI_LO = 9.67653589793e-4
INV_TWO_PI = 0.15915494309189535


def cosine(arg):
    turns = jnp.floor(arg * INV_TWO_PI + 0.5)
    half = arg * 0.5 - turns * PI_HI
    half = half - turns * PI_LO
    sq = half * half
    poly = sq * 2.6000493542416553e-06 + -0.00019806612414667135
    poly = poly * sq + 0.0083330172462401
    poly = poly * sq + -0.16666657094222279
    sine = half + half * (sq * poly)
    return 1.0 - 2.0 * (sine * sine)


def dot00(a, b):
    return lax.dot_general(a, b, (((0,), (0,)), ((), ())), preferred_element_type=F32)


def dot11(a, b):
    return lax.dot_general(a, b, (((1,), (1,)), ((), ())), preferred_element_type=F32)


def dot10(a, b):
    return lax.dot_general(a, b, (((1,), (0,)), ((), ())), preferred_element_type=F32)


def split_norm(cols):
    wide = cols.astype(F32)
    norm = jnp.sum(wide * wide, axis=0, keepdims=True) * (-1.0 / cols.shape[0])
    hi = norm.astype(BF16).astype(F32)
    rest = norm - hi
    mid = rest.astype(BF16).astype(F32)
    return hi, mid, rest - mid


def extra_rows(terms, width, first):
    rows = lax.broadcasted_iota(jnp.int32, (16, width), 0)
    out = jnp.where((rows >= 3 - first) & (rows < 6 - first), 1.0, 0.0)
    for i in range(3):
        out = jnp.where(rows == first + i, terms[i], out)
    return out.astype(BF16)


def kernel(
    nx, ny, nz, total_points, total_feats,
    bt_in, pT_in, uT_in, vT_in, ob_in, nT_in, fr_in, ph_in, wT_in,
    du, dv,
    bt, uT, vT, ob, nT, fr, ph, wT,
    gat, pa, xs1, xr1, xs2, xr2, xa, xy, pa0, kc, kk,
    pf, pr, zs, zr, vg, vy, cs, sg, fz, isem, ssem, rsem,
):
    nh = nz // 2
    ns = nx * 2
    loads = []
    for i, (src, dst) in enumerate((
        (bt_in, bt), (pT_in, gat.at[0, pl.ds(0, 32)]), (uT_in, uT), (fr_in, fr), (ph_in, ph),
        (wT_in, wT), (ob_in, ob), (nT_in, nT), (vT_in, vT),
    )):
        loads.append(pltpu.make_async_copy(src, dst, isem.at[i]))
        loads[-1].start()

    g = lax.axis_index("grp")
    f = lax.axis_index("feat")
    y = lax.div(g, 2)
    zl = lax.rem(g, 2)
    x = lax.div(f, nh * 2)
    c = lax.rem(f, 2)
    zh = lax.rem(lax.div(f, 2), nh)
    z = zh * 2 + zl
    s = x * 2 + c

    def at(s_, y_, z_):
        return {
            "grp": y_ * 2 + lax.rem(z_, 2),
            "feat": lax.div(s_, 2) * (nh * 2) + lax.div(z_, 2) * 2 + lax.rem(s_, 2),
        }

    def far_first(n):
        return sorted(range(1, n), key=lambda k: -min(k, n - k))

    block_of = {j: lax.rem(s + j, ns) for j in range(1, ns)}
    s_order = sorted(range(1, ns), key=lambda j: (-min(j, ns - j), j))
    s_dev = {j: at(block_of[j], y, z) for j in block_of}
    y_dev = {k: at(s, lax.rem(y + k, ny), z) for k in range(1, ny)}
    z_dev = {k: at(s, y, lax.rem(z + k, nz)) for k in range(1, nz)}

    barrier = pltpu.get_barrier_semaphore()
    greeted = [z_dev[k] for k in far_first(nz)] + [y_dev[k] for k in far_first(ny)]
    greeted += [s_dev[j] for j in s_order]
    for d in greeted:
        pl.semaphore_signal(barrier, inc=1, device_id=d, device_id_type=MESH)

    counts = [0, 0]
    closing = []

    def stage(copies, landing):
        i = counts[0]
        counts[0] += 1
        for src, dst, dev in copies:
            pltpu.make_async_remote_copy(
                src_ref=src, dst_ref=dst, send_sem=ssem.at[i], recv_sem=rsem.at[i],
                device_id=dev, device_id_type=MESH,
            ).start()
        whole = pltpu.make_async_remote_copy(
            src_ref=landing, dst_ref=landing, send_sem=ssem.at[i], recv_sem=rsem.at[i],
            device_id=copies[0][2], device_id_type=MESH,
        )
        closing.append(whole)
        return whole

    def owned(t):
        tile = bt[t]
        return lax.div(tile, 2) == f, lax.rem(tile, 2) == 0

    def pick(ref, low):
        return jnp.where(low, ref[:, :TILE], ref[:, TILE:])

    loads[0].wait()
    loads[1].wait()
    for t in range(STEPS):
        mine, low = owned(t)
        tile_rows = jnp.where(low, gat[0, 0:32, 0:TILE], gat[0, 0:32, TILE:])
        xs1[t] = jnp.where(mine, tile_rows.astype(F32), 0.0).astype(BF16)
    pl.semaphore_wait(barrier, len(greeted))

    hop_c = [
        stage([(xs1.at[t], xr1.at[t, j], s_dev[j]) for j in s_order], xr1.at[t, pl.ds(1, ns - 1)])
        for t in range(STEPS)
    ]
    rows_p, rows_d = pl.ds(0, 32), pl.ds(32, 64)
    others = pl.ds(1, ny - 1)
    bulk = stage(
        [(gat.at[0, rows_p], gat.at[k, rows_p], y_dev[k]) for k in far_first(ny)], gat.at[others, rows_p]
    )
    loads[2].wait()
    gat[0, 32:96, :] = uT[...].astype(BF16)
    bulk_d = stage(
        [(gat.at[0, rows_d], gat.at[k, rows_d], y_dev[k]) for k in far_first(ny)], gat.at[others, rows_d]
    )
    hop_d = []
    for t in range(STEPS):
        hop_c[t].wait_recv()
        acc = xs1[t]
        for j in range(1, ns):
            acc = acc + xr1[t, j]
        xs2[t] = acc
        hop_d.append(stage(
            [(xs2.at[t], xr2.at[t, k], z_dev[k]) for k in far_first(nz)], xr2.at[t, pl.ds(1, nz - 1)]
        ))
    for load in loads[3:]:
        load.wait()

    def build_points(k):
        block = gat[k, 0:32, :]
        pa[k, 0:32, :] = block
        pa[k, 32:48, :] = extra_rows(split_norm(block), 2 * TILE, 3)

    def batch_rows(t):
        hop_d[t].wait_recv()
        own = xs2[t]
        for k in range(2, nz, 2):
            own = own + xr2[t, k]
        oth = xr2[t, 1]
        for k in range(3, nz, 2):
            oth = oth + xr2[t, k]
        for i, rows in enumerate((own, oth)):
            lanes = slice(i * TILE, (i + 1) * TILE)
            if t == 0:
                xy[0, :, lanes] = rows
            xa[t, 0:32, lanes] = (rows.astype(F32) * (2.0 / 32)).astype(BF16)
            xa[t, 32:48, lanes] = extra_rows(split_norm(rows), TILE, 0)
        return own

    kv_scale = -step_size * amplitude / math.sqrt(total_points)
    prior_scale = -step_size * signal * math.sqrt(2.0 / total_feats)

    def prior_part(rows):
        feats = cosine(dot00(rows, fr[...]) + ph[...]).astype(BF16)
        return dot11(wT[...], feats) * prior_scale

    def kernel_part(t):
        xat = xa[t]
        if t == 0:
            for k in range(ny // 2):
                kk[k] = jnp.exp(dot00(pa[k], xat)).astype(BF16)
            bulk_d.wait_recv()
            acc = jnp.zeros((64, 2 * TILE), F32)
            for k in range(ny):
                kern = kk[k] if k < ny // 2 else jnp.exp(dot00(pa[k], xat)).astype(BF16)
                acc = acc + dot10(gat[k, 32:96, :], kern)
            return acc * kv_scale

        def one(k, acc):
            kern = jnp.exp(dot00(pa[k], xat)).astype(BF16)
            return acc + dot10(gat[k, 32:96, :], kern)

        return lax.fori_loop(0, ny, one, jnp.zeros((64, 2 * TILE), F32), unroll=True) * kv_scale

    def own_terms(t):
        mine, low = owned(t)
        terms = step_size * (pick(ob, low) - pick(nT, low))
        if t == 0:
            terms = terms + momentum * pick(vT, low)
        return jnp.where(mine, terms, 0.0)

    def partial(t, prior):
        part = kernel_part(t)
        own = part[:, :TILE] + prior
        pf[t, :, :, 0:TILE] = own.reshape(ns, 64 // ns, TILE)
        pf[t, :, :, TILE:] = part[:, TILE:].reshape(ns, 64 // ns, TILE)
        return stage(
            [(pf.at[t, block_of[j]], pr.at[t, j], s_dev[j]) for j in s_order],
            pr.at[t, pl.ds(1, ns - 1)],
        )

    def stage_z(t, hop):
        hop.wait_recv()
        share = pf[t, s]
        for j in range(1, ns):
            share = share + pr[t, j]
        hop = None
        if t == 0:
            vy[0] = share.astype(BF16)
            hop = stage([(vy.at[0], vy.at[k], y_dev[k]) for k in far_first(ny)], vy.at[pl.ds(1, ny - 1)])
        zs[t, 0] = share[:, :TILE]
        zs[t, 1] = share[:, TILE:]
        return hop, stage(
            [(zs.at[t, k % 2], zr.at[t, k], z_dev[k]) for k in far_first(nz)],
            zr.at[t, pl.ds(1, nz - 1)],
        )

    def stage_end(t, hop):
        hop.wait_recv()
        return sum((zr[t, k] for k in range(1, nz)), zs[t, 0])

    build_points(0)
    base0 = own_terms(0)
    bulk.wait_recv()
    for k in range(1, ny):
        build_points(k)
    rows0 = batch_rows(0)
    prior0 = prior_part(rows0) + base0
    hop0 = partial(0, prior0)
    hop_xy = stage([(xy.at[0], xy.at[k], y_dev[k]) for k in far_first(ny)], xy.at[pl.ds(1, ny - 1)])
    base1 = own_terms(1)
    rows1 = batch_rows(1)
    hop1 = partial(1, prior_part(rows1) + base1)
    hop_vy, hop0 = stage_z(0, hop0)
    hop1 = stage_z(1, hop1)[1]
    hop_xy.wait_recv()
    xa1 = xa[1]
    for k in range(ny):
        block = xy[k]
        pa0[k, 0:32, :] = block
        pa0[k, 32:48, :] = extra_rows(split_norm(block), 2 * TILE, 3)
        kc[k] = jnp.exp(dot00(pa0[k], xa1)).astype(BF16)

    hop_vy.wait_recv()
    corr = dot10(vy[0], kc[0])
    for k in range(1, ny):
        corr = corr + dot10(vy[k], kc[k])
    corr = (corr * kv_scale).astype(BF16)
    cs[0] = corr[:, :TILE]
    cs[1] = corr[:, TILE:]
    fz[0, s] = corr[:, :TILE]
    copies = [
        (cs.at[k % 2], fz.at[k, s], at(s if j == 0 else block_of[j], y, lax.rem(z + k, nz)))
        for j in s_order + [0] for k in far_first(nz)
    ]
    last = stage(copies, fz.at[pl.ds(1, nz - 1)])
    last_s = stage([(cs.at[0], fz.at[0, s], s_dev[j]) for j in s_order], fz.at[0, pl.ds(1, ns - 1)])

    for t, hop in enumerate((hop0, hop1)):
        share = stage_end(t, hop)
        sg[t] = share
        vg[s, t] = share
    stage([(sg, vg.at[s], s_dev[j]) for j in s_order], vg.at[pl.ds(1, ns - 1)]).wait_recv()
    new0 = vg[:, 0].reshape(64, TILE)
    mine, low = owned(0)
    for h in range(2):
        lanes = slice(h * TILE, (h + 1) * TILE)
        here = mine & (low == (h == 0))
        du[:, lanes] = jnp.where(here, new0, 0.0)
        dv[:, lanes] = jnp.where(here, new0 - vT[:, lanes], 0.0)
    mine, low = owned(1)
    kept = momentum * (pick(vT, low) + pick(dv, low))
    kept = kept + vg[:, 1].reshape(64, TILE)
    for whole in closing:
        whole.wait_send()
    last.wait_recv()
    last_s.wait_recv()
    new1 = sum((fz[k].astype(F32) for k in range(1, nz)), fz[0].astype(F32)).reshape(64, TILE) + kept
    for h in range(2):
        lanes = slice(h * TILE, (h + 1) * TILE)
        here = mine & (low == (h == 0))
        du[:, lanes] = du[:, lanes] + jnp.where(here, new1, 0.0)
        dv[:, lanes] = jnp.where(here, new1 - vT[:, lanes], dv[:, lanes])


def local(
    nx, ny, nz,
    points, dual_weights, velocity, observed, noise_draws, frequencies, phases,
    prior_weights, batch_tiles,
):
    own, samples = dual_weights.shape
    feats = phases.shape[0]
    ns = nx * 2
    stages = 15
    vm = pltpu.VMEM
    share = samples // ns
    out = vm((samples, own), F32)
    add_u, add_v = pl.pallas_call(
        functools.partial(
            kernel, nx, ny, nz, own * nx * ny * nz * 2, feats * nx * nz
        ),
        out_shape=(out, out),
        in_specs=[pl.BlockSpec(memory_space=pl.ANY)] * 9,
        out_specs=(pl.BlockSpec(memory_space=pltpu.VMEM),) * 2,
        scratch_shapes=[
            pltpu.SMEM((STEPS,), jnp.int32),
            vm((samples, own), F32),
            vm((samples, own), F32),
            vm((1, own), F32),
            vm((samples, own), F32),
            vm((32, feats), BF16),
            vm((1, feats), F32),
            vm((samples, feats), BF16),
            vm((ny, 32 + samples, own), BF16),
            vm((ny, 48, own), BF16),
            vm((STEPS, 32, TILE), BF16),
            vm((STEPS, ns, 32, TILE), BF16),
            vm((STEPS, 32, TILE), BF16),
            vm((STEPS, nz, 32, TILE), BF16),
            vm((STEPS, 48, 2 * TILE), BF16),
            vm((ny, 32, 2 * TILE), BF16),
            vm((ny, 48, 2 * TILE), BF16),
            vm((ny, 2 * TILE, 2 * TILE), BF16),
            vm((ny, own, 2 * TILE), BF16),
            vm((STEPS, ns, share, 2 * TILE), F32),
            vm((STEPS, ns, share, 2 * TILE), F32),
            vm((STEPS, 2, share, TILE), F32),
            vm((STEPS, nz, share, TILE), F32),
            vm((ns, STEPS, share, TILE), F32),
            vm((ny, share, 2 * TILE), BF16),
            vm((2, share, TILE), BF16),
            vm((STEPS, share, TILE), F32),
            vm((nz, ns, share, TILE), BF16),
            pltpu.SemaphoreType.DMA((9,)),
            pltpu.SemaphoreType.DMA((stages,)),
            pltpu.SemaphoreType.DMA((stages,)),
        ],
        compiler_params=pltpu.CompilerParams(collective_id=0, has_side_effects=True),
    )(
        batch_tiles.reshape(STEPS),
        points.T,
        dual_weights.T,
        velocity.T,
        observed.reshape(1, own),
        noise_draws.T,
        frequencies,
        phases.reshape(1, feats),
        prior_weights.T,
    )
    return dual_weights + add_u.T, velocity + add_v.T


def solution(mesh):
    nx = NX
    ny = mesh.shape["grp"] // 2
    nz = mesh.shape["feat"] // nx
    return jax.shard_map(
        functools.partial(local, nx, ny, nz),
        mesh=mesh,
        in_specs=(
            P(("grp", "feat"), None),
            P(("grp", "feat"), None),
            P(("grp", "feat"), None),
            P(("grp", "feat")),
            P(("grp", "feat"), None),
            P(None, "feat"),
            P("feat"),
            P("feat", None),
            P(None, "grp", None),
        ),
        out_specs=(P(("grp", "feat"), None), P(("grp", "feat"), None)),
        check_vma=False,
    )
```
